128 devices in a mesh: gy: 8 (over z_lo, x), gz: 16 (over y, z_hi, core).
Axes of the slice: x: 4, y: 4, z: 4 (z_hi: 2, z_lo: 2; z = z_hi * 2 + z_lo), core: 2. Of those that a mesh axis runs over, the one named last changes fastest.
Arguments:
- density: float32 [1024, 128, 256], P('gy', 'gz'), may hold values from 0.5 to 2
- momentum: float32 [3, 1024, 128, 256], P(None, 'gy', 'gz'), may hold values from -3 to 3
- energy: float32 [1024, 128, 256], P('gy', 'gz'), may hold values from 2 to 4
- wall_operator: float32 [1024, 1024], replicated, may hold values from -0.1875 to 0.1875
- span_operator: float32 [128, 128], replicated, may hold values from -0.5 to 0.5
- damping: float32 [1024], replicated, may hold values from 0.1 to 1
Outputs:
- new_density: float32 [1024, 128, 256], P('gy', 'gz')
- new_momentum: float32 [3, 1024, 128, 256], P(None, 'gy', 'gz')
- new_energy: float32 [1024, 128, 256], P('gy', 'gz')
The draws below stay inside these ranges and needn't reach their ends.
All inputs are finite; a program needn't handle non-finite values.
Results may differ from the reference program's by a relative error of at most 0.00009.
Values sent between devices are 32-bit elements; how exact they have to be, the bound alone decides.
A program may use at most 256 MiB of HBM per device.

```python
import math
import jax
import jax.numpy as jnp
from jax import lax

NY = 1024
NZ = 128
NX = 256


def block_levels(key, dims, shards, smallest, high):
    level = 1.0
    for position, blocks in shards:
        heights = jax.random.uniform(jax.random.fold_in(jax.random.fold_in(key, 6), position), (blocks,), jnp.float32, smallest / len(shards), high / len(shards))
        level = level * jnp.repeat(jnp.exp(heights), dims[position] // blocks).reshape((-1,) + (1,) * (len(dims) - 1 - position))
    return level


def centred(own_key, shape, spread, bound, cuts=(), dtype=jnp.bfloat16):
    array = jax.random.normal(own_key, shape, jnp.float32) * spread
    if len(cuts) > 0:
        array = block_levels(own_key, shape, cuts, -0.22, 0.18) * array
    return jnp.clip(array, min=-bound, max=bound).astype(dtype)


def setup_inputs(seed: int = 0) -> dict:
    seeds = jax.random.split(jax.random.key(seed), 7)
    density = jnp.clip(0.5 + 1.5 * jax.random.uniform(seeds[0], (NY, NZ, NX), jnp.float32) ** block_levels(seeds[0], (NY, NZ, NX), ((0, 8), (1, 16)), -0.2, 0.2), 0.5, 2.0)
    momentum = centred(seeds[1], (3, NY, NZ, NX), 0.7, 3.0, ((1, 8), (2, 16)), jnp.float32)
    energy = jnp.clip(2.0 + 2.0 * jax.random.uniform(seeds[2], (NY, NZ, NX), jnp.float32) ** block_levels(seeds[2], (NY, NZ, NX), ((0, 8), (1, 16)), -0.2, 0.2), 2.0, 4.0)
    wall_operator = centred(seeds[3], (NY, NY), NY ** -0.5, 0.1875, (), jnp.float32)
    span_operator = centred(seeds[4], (NZ, NZ), NZ ** -0.5, 0.5, (), jnp.float32)
    damping = jnp.clip(jnp.exp(jax.random.uniform(seeds[5], (NY,), jnp.float32, math.log(0.1), math.log(1.0))), 0.1, 1.0)
    return dict(density=density, momentum=momentum, energy=energy, wall_operator=wall_operator, span_operator=span_operator, damping=damping)


gamma_less = 0.4
time_step = 0.1


def flux_along(conserved, direction):
    velocity = conserved[1 + direction] / conserved[0]
    kinetic = 0.5 * (conserved[1] * conserved[1] + conserved[2] * conserved[2] + conserved[3] * conserved[3]) / conserved[0]
    pressure = gamma_less * (conserved[4] - kinetic)
    components = [conserved[1 + direction]]
    for column in range(3):
        product = conserved[1 + column] * velocity
        if column == direction:
            product = product + pressure
        components.append(product)
    components.append((conserved[4] + pressure) * velocity)
    return jnp.stack(components)


def x_derivative(flux_field):
    widths = [(0, 0)] * (flux_field.ndim - 1) + [(2, 2)]
    padded = jnp.pad(flux_field, widths, mode="edge")
    return (8.0 * (padded[..., 3:-1] - padded[..., 1:-3]) - (padded[..., 4:] - padded[..., :-4])) / 12.0


def fourth_difference(padded, along_axis, length_out):
    def shifted(offset):
        return lax.slice_in_dim(padded, offset, offset + length_out, axis=along_axis)
    return shifted(0) - 4.0 * shifted(1) + 6.0 * shifted(2) - 4.0 * shifted(3) + shifted(4)


def reference(density, momentum, energy, wall_operator, span_operator, damping):
    conserved = jnp.concatenate([density[None], momentum, energy[None]], axis=0)

    def plane_part(one_plane):
        across = flux_along(one_plane, 0)
        upward = flux_along(one_plane, 1)
        deriv_y = jnp.einsum("ij,fjx->fix", wall_operator, upward, precision=lax.Precision.HIGHEST)
        padded = jnp.pad(one_plane, ((0, 0), (2, 2), (0, 0)))
        return -x_derivative(across) - deriv_y - damping[None, :, None] * fourth_difference(padded, 1, NY)

    planes = lax.map(plane_part, jnp.moveaxis(conserved, 2, 0))
    plane_terms = jnp.moveaxis(planes, 0, 2)

    def row_part(inputs):
        one_row, weight = inputs
        sideways = flux_along(one_row, 2)
        deriv_z = jnp.einsum("ij,fjx->fix", span_operator, sideways, precision=lax.Precision.HIGHEST)
        padded = jnp.concatenate([one_row[:, -2:], one_row, one_row[:, :2]], axis=1)
        return -deriv_z - weight * fourth_difference(padded, 1, NZ)

    rows_out = lax.map(row_part, (jnp.moveaxis(conserved, 1, 0), damping))
    row_terms = jnp.moveaxis(rows_out, 0, 1)
    advanced = conserved + time_step * (plane_terms + row_terms)
    return advanced[0], advanced[1:4], advanced[4]
```

```python
import functools

import jax
import jax.numpy as jnp
import numpy as np
from jax import lax
from jax.experimental import pallas as pl
from jax.experimental.pallas import tpu as pltpu
from jax.sharding import PartitionSpec as P

MESH = pl.DeviceIdType.MESH
GAMMA_LESS = 0.4
TIME_STEP = 0.1
GY, GZ = 8, 16
ROWS, PLANES, CELLS, LANES = 128, 8, 256, 128
NY, NZ = GY * ROWS, GZ * PLANES
HOLD = ROWS // GZ
PAD = 8


def flux_along(c, direction):
    inverse = 1.0 / c[0]
    velocity = c[1 + direction] * inverse
    kinetic = 0.5 * (c[1] * c[1] + c[2] * c[2] + c[3] * c[3]) * inverse
    pressure = GAMMA_LESS * (c[4] - kinetic)
    out = [c[1 + direction]]
    for column in range(3):
        product = c[1 + column] * velocity
        if column == direction:
            product = product + pressure
        out.append(product)
    out.append((c[4] + pressure) * velocity)
    return out


def split(x):
    high = x.astype(jnp.bfloat16)
    low = (x - high.astype(jnp.float32)).astype(jnp.bfloat16)
    return high, low


def dot(a, b):
    return jnp.dot(a, b, preferred_element_type=jnp.float32)


def exchange(
    dens, mom, ene, wall, span, damp, damp_rows, fourth,
    dy_out, dz_out,
    own, lines_y, lines_z, by_plane, dy_send, dz_send, wall_f, wall_h, wall_l, flux_h, flux_l, span_3,
    ysend, yrecv, zsend, zrecv, ysend2, yrecv2, zsend2, zrecv2, local_sem,
):
    gy = lax.axis_index("gy")
    gz = lax.axis_index("gz")
    y_peers = [(lax.rem(gy + d, GY), gz) for d in range(1, GY)]
    z_peers = [(gy, lax.rem(gz + d, GZ)) for d in range(1, GZ)]

    loads = []
    for h in range(2):
        lanes = pl.ds(h * LANES, LANES)
        loads += [
            pltpu.make_async_copy(dens.at[:, lanes], own.at[h, 0], local_sem.at[3 * h]),
            pltpu.make_async_copy(mom.at[:, :, lanes], own.at[h, pl.ds(1, 3)], local_sem.at[3 * h + 1]),
            pltpu.make_async_copy(ene.at[:, lanes], own.at[h, 4], local_sem.at[3 * h + 2]),
        ]
    load_wall = pltpu.make_async_copy(wall, wall_f, local_sem.at[6])
    for copy in loads:
        copy.start()
    load_wall.start()

    barrier = pltpu.get_barrier_semaphore()
    for peer in y_peers + z_peers:
        pl.semaphore_signal(barrier, inc=1, device_id=peer, device_id_type=MESH)
    for copy in loads:
        copy.wait()

    @pl.loop(0, 5)
    def _(f):
        for p in range(PLANES):
            for h in range(2):
                by_plane[p, h, f] = own[h, f, pl.ds(p, ROWS, stride=PLANES), :]

    pl.semaphore_wait(barrier, GY + GZ - 2)

    y_out = []
    for d in range(1, GY):
        peer = y_peers[d - 1]
        y_out.append(
            pltpu.make_async_remote_copy(
                by_plane.at[peer[0]],
                lines_y.at[:, :, pl.ds(PAD + gy * ROWS, ROWS), :],
                ysend.at[d - 1], yrecv.at[d - 1], device_id=peer, device_id_type=MESH,
            )
        )
    z_out = []
    for d in range(1, GZ):
        peer = z_peers[d - 1]
        z_out.append(
            pltpu.make_async_remote_copy(
                own.at[:, :, pl.ds(peer[1] * (HOLD * PLANES), HOLD * PLANES), :],
                lines_z.at[gz],
                zsend.at[d - 1], zrecv.at[d - 1], device_id=peer, device_id_type=MESH,
            )
        )
    for copy in y_out:
        copy.start()
    for copy in z_out:
        copy.start()
    keep = [
        pltpu.make_async_copy(by_plane.at[gy], lines_y.at[:, :, pl.ds(PAD + gy * ROWS, ROWS), :], local_sem.at[4]),
        pltpu.make_async_copy(own.at[:, :, pl.ds(gz * (HOLD * PLANES), HOLD * PLANES), :], lines_z.at[gz], local_sem.at[5]),
    ]
    for copy in keep:
        copy.start()

    load_wall.wait()

    @pl.loop(0, NY // 64)
    def _(i):
        rows = pl.ds(i * 64, 64)
        high, low = split(wall_f[rows, :])
        wall_h[rows, :] = high
        wall_l[rows, :] = low

    high, low = split(span[...])
    span_3[:, 0:NZ] = high
    span_3[:, NZ : 2 * NZ] = high
    span_3[:, 2 * NZ : 3 * NZ] = low
    for h in range(2):
        for f in range(5):
            lines_y[h, f, 0:PAD, :] = jnp.zeros((PAD, LANES), jnp.float32)
            lines_y[h, f, PAD + NY : 2 * PAD + NY, :] = jnp.zeros((PAD, LANES), jnp.float32)

    keep[0].wait()
    for copy in y_out:
        copy.wait_recv()

    for h in range(2):

        @pl.loop(0, NY // 64)
        def _(i):
            r = pl.multiple_of(i * 64, 64)
            c = [lines_y[h, f, pl.ds(PAD + r, 64), :] for f in range(5)]
            for f, value in enumerate(flux_along(c, 1)):
                high, low = split(value)
                flux_h[pl.ds(r, 64), f * LANES : (f + 1) * LANES] = high
                flux_l[pl.ds(r, 64), f * LANES : (f + 1) * LANES] = low

        @pl.loop(0, GY)
        def _(g):
            r = pl.multiple_of(g * ROWS, ROWS)
            rows = pl.ds(r, ROWS)
            total = dot(wall_h[rows, :], flux_h[...])
            total += dot(wall_h[rows, :], flux_l[...])
            total += dot(wall_l[rows, :], flux_h[...])
            weight = damp_rows[rows, :]
            for f in range(5):
                window = lines_y[h, f, pl.ds(r, ROWS + 2 * PAD), :]

                def at(k, window=window):
                    return window[PAD + k : PAD + k + ROWS]

                smooth = at(-2) - 4.0 * at(-1) + 6.0 * at(0) - 4.0 * at(1) + at(2)
                dy_send[g, h, f] = total[:, f * LANES : (f + 1) * LANES] + weight * smooth

    y_back = []
    for d in range(1, GY):
        peer = y_peers[d - 1]
        y_back.append(
            pltpu.make_async_remote_copy(
                dy_send.at[peer[0]], dy_out.at[gy],
                ysend2.at[d - 1], yrecv2.at[d - 1], device_id=peer, device_id_type=MESH,
            )
        )
        y_back[-1].start()
    keep_y = pltpu.make_async_copy(dy_send.at[gy], dy_out.at[gy], local_sem.at[0])
    keep_y.start()

    keep[1].wait()
    for copy in z_out:
        copy.wait_recv()

    @pl.loop(0, HOLD)
    def _(r):
        at = pl.ds(pl.multiple_of(r * PLANES, PLANES), PLANES)
        weight = damp[gy * ROWS + gz * HOLD + r]
        for h in range(2):
            c = [lines_z[:, h, f, at, :].reshape(NZ, LANES) for f in range(5)]
            high, low = split(jnp.concatenate(flux_along(c, 2), axis=1))
            total = dot(span_3[...], jnp.concatenate([high, low, high], axis=0))
            high, low = split(jnp.concatenate(c, axis=1))
            total += weight * dot(fourth[...], jnp.concatenate([high, low], axis=0))
            for f in range(5):
                dz_send[:, h, f, at, :] = total[:, f * LANES : (f + 1) * LANES].reshape(GZ, PLANES, LANES)

    z_back = []
    for d in range(1, GZ):
        peer = z_peers[d - 1]
        z_back.append(
            pltpu.make_async_remote_copy(
                dz_send.at[peer[1]], dz_out.at[:, :, pl.ds(gz * (HOLD * PLANES), HOLD * PLANES), :],
                zsend2.at[d - 1], zrecv2.at[d - 1], device_id=peer, device_id_type=MESH,
            )
        )
        z_back[-1].start()
    keep_z = pltpu.make_async_copy(
        dz_send.at[gz], dz_out.at[:, :, pl.ds(gz * (HOLD * PLANES), HOLD * PLANES), :], local_sem.at[1]
    )
    keep_z.start()
    keep_y.wait()
    keep_z.wait()
    for copy in y_out + z_out:
        copy.wait_send()
    for copy in y_back + z_back:
        copy.wait()


def finish(dens, mom, ene, dy, dz, shift, new_dens, new_mom, new_ene, turned):
    c = [dens[...], mom[0], mom[1], mom[2], ene[...]]
    count = dens.shape[0] // PLANES
    for h in range(2):
        for f in range(5):
            for p in range(PLANES):
                turned[h, f, pl.ds(p, count, stride=PLANES), :] = dy[p, h, f]
    for f, value in enumerate(flux_along(c, 0)):
        high, low = split(value)
        along = (dot(high, shift[...]) + dot(low, shift[...])) * (1.0 / 12.0)
        across = jnp.concatenate([turned[h, f] + dz[h, f] for h in range(2)], axis=1)
        value = c[f] - TIME_STEP * (along + across)
        if f == 0:
            new_dens[...] = value
        elif f == 4:
            new_ene[...] = value
        else:
            new_mom[f - 1] = value


def fourth_matrix():
    m = np.zeros((NZ, NZ), np.float32)
    for i in range(NZ):
        for k, w in ((-2, 1.0), (-1, -4.0), (0, 6.0), (1, -4.0), (2, 1.0)):
            m[i, (i + k) % NZ] += w
    return np.concatenate([m, m], axis=1)


def shift_matrix():
    m = np.zeros((CELLS, CELLS), np.float32)
    for i in range(CELLS):
        for k, w in ((1, 8.0), (-1, -8.0), (2, -1.0), (-2, 1.0)):
            m[min(max(i + k, 0), CELLS - 1), i] += w
    return m


ANY = pl.BlockSpec(memory_space=pl.ANY)
VMEM = pl.BlockSpec(memory_space=pltpu.VMEM)
DMA = pltpu.SemaphoreType.DMA


def local(density, momentum, energy, wall_operator, span_operator, damping):
    cells = ROWS * PLANES
    dens = density.reshape(cells, CELLS)
    mom = momentum.reshape(3, cells, CELLS)
    ene = energy.reshape(cells, CELLS)
    f32, bf16 = jnp.float32, jnp.bfloat16
    dy, dz = pl.pallas_call(
        exchange,
        out_shape=(
            jax.ShapeDtypeStruct((PLANES, 2, 5, ROWS, LANES), f32),
            jax.ShapeDtypeStruct((2, 5, cells, LANES), f32),
        ),
        in_specs=[ANY, ANY, ANY, ANY, VMEM, pl.BlockSpec(memory_space=pltpu.SMEM), VMEM, VMEM],
        out_specs=(ANY, ANY),
        scratch_shapes=[
            pltpu.VMEM((2, 5, cells, LANES), f32),
            pltpu.VMEM((2, 5, NY + 2 * PAD, LANES), f32),
            pltpu.VMEM((GZ, 2, 5, HOLD * PLANES, LANES), f32),
            pltpu.VMEM((PLANES, 2, 5, ROWS, LANES), f32),
            pltpu.VMEM((GY, 2, 5, ROWS, LANES), f32),
            pltpu.VMEM((GZ, 2, 5, HOLD * PLANES, LANES), f32),
            pltpu.VMEM((NY, NY), f32),
            pltpu.VMEM((NY, NY), bf16),
            pltpu.VMEM((NY, NY), bf16),
            pltpu.VMEM((NY, 5 * LANES), bf16),
            pltpu.VMEM((NY, 5 * LANES), bf16),
            pltpu.VMEM((NZ, 3 * NZ), bf16),
            DMA((GY - 1,)), DMA((GY - 1,)), DMA((GZ - 1,)), DMA((GZ - 1,)),
            DMA((GY - 1,)), DMA((GY - 1,)), DMA((GZ - 1,)), DMA((GZ - 1,)),
            DMA((7,)),
        ],
        compiler_params=pltpu.CompilerParams(
            collective_id=0, has_side_effects=True, vmem_limit_bytes=62 << 20
        ),
        name="exchange",
    )(
        dens, mom, ene, wall_operator, span_operator, damping,
        jnp.broadcast_to(damping[:, None], (NY, LANES)),
        jnp.asarray(fourth_matrix(), bf16),
    )
    steps = 16
    block = cells // steps
    field = pl.BlockSpec((block, CELLS), lambda i: (i, 0))
    three = pl.BlockSpec((3, block, CELLS), lambda i: (0, i, 0))
    five = pl.BlockSpec((2, 5, block, LANES), lambda i: (0, 0, i, 0))
    new = pl.pallas_call(
        finish,
        grid=(steps,),
        out_shape=(
            jax.ShapeDtypeStruct((cells, CELLS), f32),
            jax.ShapeDtypeStruct((3, cells, CELLS), f32),
            jax.ShapeDtypeStruct((cells, CELLS), f32),
        ),
        in_specs=[
            field, three, field,
            pl.BlockSpec((PLANES, 2, 5, ROWS // steps, LANES), lambda i: (0, 0, 0, i, 0)),
            five,
            pl.BlockSpec((CELLS, CELLS), lambda i: (0, 0)),
        ],
        out_specs=(field, three, field),
        scratch_shapes=[pltpu.VMEM((2, 5, block, LANES), f32)],
        name="finish",
    )(dens, mom, ene, dy, dz, jnp.asarray(shift_matrix(), bf16))
    shape = (ROWS, PLANES, CELLS)
    return new[0].reshape(shape), new[1].reshape((3,) + shape), new[2].reshape(shape)


def solution(mesh):
    in_specs = (P("gy", "gz", None), P(None, "gy", "gz", None), P("gy", "gz", None), P(), P(), P())
    out_specs = (P("gy", "gz", None), P(None, "gy", "gz", None), P("gy", "gz", None))
    return jax.shard_map(local, mesh=mesh, in_specs=in_specs, out_specs=out_specs, check_vma=False)
```

```python
import functools

import jax
import jax.numpy as jnp
import numpy as np
from jax import lax
from jax.experimental import pallas as pl
from jax.experimental.pallas import tpu as pltpu
from jax.sharding import PartitionSpec as P

MESH = pl.DeviceIdType.MESH
GAMMA_LESS = 0.4
TIME_STEP = 0.1
GY, GZ = 8, 16
ROWS, PLANES, CELLS, LANES = 128, 8, 256, 128
NY, NZ = GY * ROWS, GZ * PLANES
HOLD = 16
CHUNKS = 4
HALF = NY // 2
PAD = 8


def flux_along(c, direction):
    inverse = 1.0 / c[0]
    velocity = c[1 + direction] * inverse
    kinetic = 0.5 * (c[1] * c[1] + c[2] * c[2] + c[3] * c[3]) * inverse
    pressure = GAMMA_LESS * (c[4] - kinetic)
    out = [c[1 + direction]]
    for column in range(3):
        product = c[1 + column] * velocity
        if column == direction:
            product = product + pressure
        out.append(product)
    out.append((c[4] + pressure) * velocity)
    return out


def split(x):
    high = x.astype(jnp.bfloat16)
    low = (x - high.astype(jnp.float32)).astype(jnp.bfloat16)
    return high, low


def dot(a, b):
    return jnp.dot(a, b, preferred_element_type=jnp.float32)


def exchange(
    dens, mom, ene, wall, span, damp, damp_rows, fourth, order_in, order_out, shift,
    dy_out, dz_out, base_out, near, far,
    own, apart, lines_y, lines_z, dy_send, dz_send, wall_f, wall_h, wall_l, flux_h, flux_l, span_3,
    z1s, z1r, z2s, z2r, x1s, x1r, x2s, x2r, x3s, x3r, y1s, y1r, y2s, y2r, y3s, y3r, load_sem, keep_sem,
):
    gy = lax.axis_index("gy")
    gz = lax.axis_index("gz")
    z_lo, x = gy // 4, lax.rem(gy, 4)
    y, z_hi, core = gz // 4, lax.rem(gz // 2, 2), lax.rem(gz, 2)
    slot = y * 2 + core
    pair = ((1 - z_lo) * 4 + x, gz)
    relay = ((1 - z_lo) * 4 + x, y * 4 + (1 - z_hi) * 2 + core)
    x_of = [lax.rem(x + d, 4) for d in range(4)]
    x_peers = [(z_lo * 4 + other, gz) for other in x_of]
    slot_of = [lax.rem(slot + d, 8) for d in range(8)]
    y_peers = [(gy, (other // 2) * 4 + z_hi * 2 + lax.rem(other, 2)) for other in slot_of]
    far_gz = y * 4 + (1 - z_hi) * 2 + core
    near_row = PAD + gy * ROWS
    far_row = PAD + pair[0] * ROWS

    def send(src, dst, ssem, rsem, peer):
        return pltpu.make_async_remote_copy(src, dst, ssem, rsem, device_id=peer, device_id_type=MESH)

    loads = []
    for h in range(2):
        lanes = pl.ds(h * LANES, LANES)
        loads += [
            pltpu.make_async_copy(dens.at[:, lanes], own.at[h, 0], load_sem.at[3 * h]),
            pltpu.make_async_copy(mom.at[:, :, lanes], own.at[h, pl.ds(1, 3)], load_sem.at[3 * h + 1]),
            pltpu.make_async_copy(ene.at[:, lanes], own.at[h, 4], load_sem.at[3 * h + 2]),
        ]
    load_wall = pltpu.make_async_copy(wall.at[pl.ds(z_lo * HALF, HALF), :], wall_f, load_sem.at[6])
    for copy in loads:
        copy.start()
    load_wall.start()

    barrier = pltpu.get_barrier_semaphore()
    for peer in [pair, relay] + x_peers[1:] + y_peers[1:]:
        pl.semaphore_signal(barrier, inc=1, device_id=peer, device_id_type=MESH)

    z1 = [send(apart.at[u], near.at[u], z1s.at[u], z1r.at[u], pair) for u in range(CHUNKS)]
    z2 = [send(near.at[u], far.at[u], z2s.at[u], z2r.at[u], relay) for u in range(CHUNKS)]
    x1, x2, x3, keeps = [], [], [], []
    for u in range(CHUNKS):
        for copies, source, row, ssem, rsem in ((x1, apart, near_row, x1s, x1r), (x2, near, far_row, x2s, x2r)):
            target = lines_y.at[u, :, pl.ds(row, ROWS), :]
            copies.append(
                [
                    send(source.at[u, x_of[d]], target, ssem.at[u, d - 1], rsem.at[u, d - 1], x_peers[d])
                    for d in range(1, 4)
                ]
            )
        x3.append(
            [
                send(dy_send.at[u, x_of[d]], dy_out.at[u, x], x3s.at[u, d - 1], x3r.at[u, d - 1], x_peers[d])
                for d in range(1, 4)
            ]
        )
        keeps.append(
            [
                pltpu.make_async_copy(apart.at[u, x], lines_y.at[u, :, pl.ds(near_row, ROWS), :], keep_sem.at[u, 0]),
                pltpu.make_async_copy(near.at[u, x], lines_y.at[u, :, pl.ds(far_row, ROWS), :], keep_sem.at[u, 1]),
                pltpu.make_async_copy(
                    apart.at[u, :, :, pl.ds(slot * HOLD, HOLD), :], lines_z.at[u, gz], keep_sem.at[u, 2]
                ),
                pltpu.make_async_copy(
                    far.at[u, :, :, pl.ds(slot * HOLD, HOLD), :], lines_z.at[u, far_gz], keep_sem.at[u, 3]
                ),
                pltpu.make_async_copy(dy_send.at[u, x], dy_out.at[u, x], keep_sem.at[u, 4]),
            ]
        )
    y1, y2, y3, keep_dz = [], [], [], []
    for u in range(CHUNKS):
        for copies, source, index, ssem, rsem in ((y1, apart, gz, y1s, y1r), (y2, far, far_gz, y2s, y2r)):
            copies.append(
                [
                    send(
                        source.at[u, :, :, pl.ds(slot_of[d] * HOLD, HOLD), :], lines_z.at[u, index],
                        ssem.at[u, d - 1], rsem.at[u, d - 1], y_peers[d],
                    )
                    for d in range(1, 8)
                ]
            )
    for h in range(2):
        home = dz_out.at[pl.ds(2 * h, 2), :, :, pl.ds(slot * HOLD, HOLD), :]
        y3.append(
            [
                send(dz_send.at[h, :, slot_of[d]], home, y3s.at[h, d - 1], y3r.at[h, d - 1], y_peers[d])
                for d in range(1, 8)
            ]
        )
        keep_dz.append(pltpu.make_async_copy(dz_send.at[h, :, slot], home, keep_sem.at[h, 5]))

    for copy in loads:
        copy.wait()
    for u in range(CHUNKS):
        h, e = u // 2, u % 2

        @pl.loop(0, 5)
        def _(f):
            for k in range(4):
                apart[u, k, f] = own[h, f, pl.ds(2 * k + e, ROWS, stride=PLANES), :]

        if u == 0:
            pl.semaphore_wait(barrier, 12)
        z1[u].start()
        for copy in x1[u]:
            copy.start()
        for copy in y1[u]:
            copy.start()
        keeps[u][0].start()
        keeps[u][2].start()

    load_wall.wait()

    @pl.loop(0, HALF // 64)
    def _(i):
        rows = pl.ds(i * 64, 64)
        high, low = split(wall_f[rows, :])
        wall_h[rows, :] = high
        wall_l[rows, :] = low

    high, low = [
        dot(order_out[z_hi], dot(part, order_in[...]).astype(jnp.bfloat16)).astype(jnp.bfloat16) for part in split(span[...])
    ]
    span_3[:, 0:NZ] = high
    span_3[:, NZ : 2 * NZ] = high
    span_3[:, 2 * NZ : 3 * NZ] = low
    for u in range(CHUNKS):
        for f in range(5):
            lines_y[u, f, 0:PAD, :] = jnp.zeros((PAD, LANES), jnp.float32)
            lines_y[u, f, PAD + NY : 2 * PAD + NY, :] = jnp.zeros((PAD, LANES), jnp.float32)

    @pl.loop(0, ROWS * PLANES // 64)
    def _(i):
        rows = pl.ds(i * 64, 64)
        c = [jnp.concatenate([own[0, f, rows, :], own[1, f, rows, :]], axis=1) for f in range(5)]
        for f, value in enumerate(flux_along(c, 0)):
            high, low = split(value)
            along = (dot(high, shift[...]) + dot(low, shift[...])) * (1.0 / 12.0)
            value = c[f] - TIME_STEP * along
            for h in range(2):
                own[h, f, rows, :] = value[:, h * LANES : (h + 1) * LANES]

    save = pltpu.make_async_copy(own, base_out, load_sem.at[0])
    save.start()

    def pass_near(u):
        z1[u].wait_recv()
        z2[u].start()
        for copy in x2[u]:
            copy.start()
        keeps[u][1].start()

    def pass_far(u):
        z2[u].wait_recv()
        for copy in y2[u]:
            copy.start()
        keeps[u][3].start()

    def derive_y(u):
        keeps[u][0].wait()
        keeps[u][1].wait()
        for copy in x1[u] + x2[u]:
            copy.wait_recv()

        @pl.loop(0, NY // 64)
        def _(i):
            r = pl.multiple_of(i * 64, 64)
            c = [lines_y[u, f, pl.ds(PAD + r, 64), :] for f in range(5)]
            for f, value in enumerate(flux_along(c, 1)):
                high, low = split(value)
                flux_h[pl.ds(r, 64), f * LANES : (f + 1) * LANES] = high
                flux_l[pl.ds(r, 64), f * LANES : (f + 1) * LANES] = low

        @pl.loop(0, 4)
        def _(k):
            rows = pl.ds(pl.multiple_of(k * ROWS, ROWS), ROWS)
            total = dot(wall_h[rows, :], flux_h[...])
            total += dot(wall_h[rows, :], flux_l[...])
            total += dot(wall_l[rows, :], flux_h[...])
            block = z_lo * 4 + k
            weight = jnp.broadcast_to(damp_rows[pl.ds(block, 1), :], (ROWS, LANES)).T
            for f in range(5):
                window = lines_y[u, f, pl.ds(pl.multiple_of(block * ROWS, ROWS), ROWS + 2 * PAD), :]

                def at(step, window=window):
                    return window[PAD + step : PAD + step + ROWS]

                smooth = at(-2) - 4.0 * at(-1) + 6.0 * at(0) - 4.0 * at(1) + at(2)
                dy_send[u, k, f] = total[:, f * LANES : (f + 1) * LANES] + weight * smooth

        for copy in x3[u]:
            copy.start()
        keeps[u][4].start()

    def derive_z(h):
        for u in (2 * h, 2 * h + 1):
            keeps[u][2].wait()
            keeps[u][3].wait()
            for copy in y1[u] + y2[u]:
                copy.wait_recv()
        lines = lines_z.reshape(CHUNKS, GZ * 4 * 5 * HOLD, LANES)
        results = dz_send.reshape(2, 2 * 8 * 4 * 5 * HOLD, LANES)

        @pl.loop(0, HOLD)
        def _(r):
            weight = damp[gy * ROWS + slot * HOLD + r]
            c = []
            for f in range(5):
                at = pl.ds(f * HOLD + r, NZ // 2, stride=5 * HOLD)
                c.append(jnp.concatenate([lines[2 * h, at, :], lines[2 * h + 1, at, :]], axis=0))
            high, low = split(jnp.concatenate(flux_along(c, 2), axis=1))
            total = dot(span_3[...], jnp.concatenate([high, low, high], axis=0))
            high, low = split(jnp.concatenate(c, axis=1))
            total += weight * dot(fourth[z_hi], jnp.concatenate([high, low], axis=0))
            for f in range(5):
                at = pl.ds(f * HOLD + r, NZ // 2, stride=5 * HOLD)
                results[h, at, :] = total[:, f * LANES : (f + 1) * LANES]

        for copy in y3[h]:
            copy.start()
        keep_dz[h].start()

    pass_near(0)
    pass_near(1)
    pass_far(0)
    derive_y(0)
    pass_near(2)
    pass_far(1)
    derive_y(1)
    derive_z(0)
    pass_near(3)
    pass_far(2)
    derive_y(2)
    pass_far(3)
    derive_y(3)
    derive_z(1)

    save.wait()
    for u in range(CHUNKS):
        z1[u].wait_send()
        z2[u].wait_send()
        keeps[u][4].wait()
        for copy in x1[u] + x2[u] + y1[u] + y2[u]:
            copy.wait_send()
        for copy in x3[u]:
            copy.wait()
    for h in range(2):
        keep_dz[h].wait()
        for copy in y3[h]:
            copy.wait()


def finish(base, dy, dz, new_dens, new_mom, new_ene, turned):
    count = new_dens.shape[0] // PLANES
    for f in range(5):
        halves = []
        for h in range(2):
            for e in range(2):
                for k in range(4):
                    u = 2 * h + e
                    turned[h, f, pl.ds(2 * k + e, count, stride=PLANES), :] = dy[u, k, f] + dz[u, k, f]
            halves.append(base[h, f] - TIME_STEP * turned[h, f])
        value = jnp.concatenate(halves, axis=1)
        if f == 0:
            new_dens[...] = value
        elif f == 4:
            new_ene[...] = value
        else:
            new_mom[f - 1] = value


def plane_order():
    return np.arange(NZ).reshape(GZ, 4, 2).transpose(2, 0, 1).reshape(-1)


def half_order(z_hi):
    return np.arange(NZ).reshape(4, 2, 2, 4, 2)[:, z_hi].transpose(3, 0, 1, 2).reshape(-1)


def order_matrices():
    eye = np.eye(NZ, dtype=np.float32)
    return eye[:, plane_order()], np.stack([eye[half_order(z)] for z in range(2)])


def fourth_matrix():
    m = np.zeros((NZ, NZ), np.float32)
    for i in range(NZ):
        for k, w in ((-2, 1.0), (-1, -4.0), (0, 6.0), (1, -4.0), (2, 1.0)):
            m[i, (i + k) % NZ] += w
    m = np.stack([m[half_order(z)][:, plane_order()] for z in range(2)])
    return np.concatenate([m, m], axis=2)


def shift_matrix():
    m = np.zeros((CELLS, CELLS), np.float32)
    for i in range(CELLS):
        for k, w in ((1, 8.0), (-1, -8.0), (2, -1.0), (-2, 1.0)):
            m[min(max(i + k, 0), CELLS - 1), i] += w
    return m


ANY = pl.BlockSpec(memory_space=pl.ANY)
VMEM = pl.BlockSpec(memory_space=pltpu.VMEM)
SMEM = pl.BlockSpec(memory_space=pltpu.SMEM)
DMA = pltpu.SemaphoreType.DMA


def local(density, momentum, energy, wall_operator, span_operator, damping):
    cells = ROWS * PLANES
    dens = density.reshape(cells, CELLS)
    mom = momentum.reshape(3, cells, CELLS)
    ene = energy.reshape(cells, CELLS)
    f32, bf16 = jnp.float32, jnp.bfloat16
    order_in, order_out = order_matrices()
    whole = jax.ShapeDtypeStruct((CHUNKS, 4, 5, ROWS, LANES), f32)
    dy, dz, base, _, _ = pl.pallas_call(
        exchange,
        out_shape=(whole, whole, jax.ShapeDtypeStruct((2, 5, cells, LANES), f32), whole, whole),
        in_specs=[ANY, ANY, ANY, ANY, VMEM, SMEM, VMEM, VMEM, VMEM, VMEM, VMEM],
        out_specs=(ANY,) * 5,
        scratch_shapes=[
            pltpu.VMEM((2, 5, cells, LANES), f32),
            pltpu.VMEM((CHUNKS, 4, 5, ROWS, LANES), f32),
            pltpu.VMEM((CHUNKS, 5, NY + 2 * PAD, LANES), f32),
            pltpu.VMEM((CHUNKS, GZ, 4, 5, HOLD, LANES), f32),
            pltpu.VMEM((CHUNKS, 4, 5, ROWS, LANES), f32),
            pltpu.VMEM((2, 2, 8, 4, 5, HOLD, LANES), f32),
            pltpu.VMEM((HALF, NY), f32),
            pltpu.VMEM((HALF, NY), bf16),
            pltpu.VMEM((HALF, NY), bf16),
            pltpu.VMEM((NY, 5 * LANES), bf16),
            pltpu.VMEM((NY, 5 * LANES), bf16),
            pltpu.VMEM((NZ // 2, 3 * NZ), bf16),
            *[DMA((CHUNKS,))] * 4,
            *[DMA((CHUNKS, 3))] * 6,
            *[DMA((CHUNKS, 7))] * 4,
            *[DMA((2, 7))] * 2,
            DMA((7,)),
            DMA((CHUNKS, 6)),
        ],
        compiler_params=pltpu.CompilerParams(
            collective_id=0, has_side_effects=True, vmem_limit_bytes=62 << 20
        ),
        name="exchange",
    )(
        dens, mom, ene, wall_operator, span_operator, damping, damping.reshape(GY, ROWS),
        jnp.asarray(fourth_matrix(), bf16), jnp.asarray(order_in, bf16), jnp.asarray(order_out, bf16),
        jnp.asarray(shift_matrix(), bf16),
    )
    steps = 16
    block = cells // steps
    field = pl.BlockSpec((block, CELLS), lambda i: (i, 0))
    three = pl.BlockSpec((3, block, CELLS), lambda i: (0, i, 0))
    apart = pl.BlockSpec((CHUNKS, 4, 5, ROWS // steps, LANES), lambda i: (0, 0, 0, i, 0))
    new = pl.pallas_call(
        finish,
        grid=(steps,),
        out_shape=(
            jax.ShapeDtypeStruct((cells, CELLS), f32),
            jax.ShapeDtypeStruct((3, cells, CELLS), f32),
            jax.ShapeDtypeStruct((cells, CELLS), f32),
        ),
        in_specs=[pl.BlockSpec((2, 5, block, LANES), lambda i: (0, 0, i, 0)), apart, apart],
        out_specs=(field, three, field),
        scratch_shapes=[pltpu.VMEM((2, 5, block, LANES), f32)],
        name="finish",
    )(base, dy, dz)
    shape = (ROWS, PLANES, CELLS)
    return new[0].reshape(shape), new[1].reshape((3,) + shape), new[2].reshape(shape)


def solution(mesh):
    in_specs = (P("gy", "gz", None), P(None, "gy", "gz", None), P("gy", "gz", None), P(), P(), P())
    out_specs = (P("gy", "gz", None), P(None, "gy", "gz", None), P("gy", "gz", None))
    return jax.shard_map(local, mesh=mesh, in_specs=in_specs, out_specs=out_specs, check_vma=False)
```

```python
import functools

import jax
import jax.numpy as jnp
import numpy as np
from jax import lax
from jax.experimental import pallas as pl
from jax.experimental.pallas import tpu as pltpu
from jax.sharding import PartitionSpec as P

MESH = pl.DeviceIdType.MESH
GAMMA_LESS = 0.4
TIME_STEP = 0.1
GY, GZ = 8, 16
ROWS, PLANES, CELLS, LANES = 128, 8, 256, 128
NY, NZ = GY * ROWS, GZ * PLANES
HOLD = 16
CHUNKS = 4
HALF = NY // 2
PAD = 8


def flux_along(c, direction):
    inverse = 1.0 / c[0]
    velocity = c[1 + direction] * inverse
    kinetic = 0.5 * (c[1] * c[1] + c[2] * c[2] + c[3] * c[3]) * inverse
    pressure = GAMMA_LESS * (c[4] - kinetic)
    out = [c[1 + direction]]
    for column in range(3):
        product = c[1 + column] * velocity
        if column == direction:
            product = product + pressure
        out.append(product)
    out.append((c[4] + pressure) * velocity)
    return out


def split(x):
    high = x.astype(jnp.bfloat16)
    low = (x - high.astype(jnp.float32)).astype(jnp.bfloat16)
    return high, low


def dot(a, b):
    return jnp.dot(a, b, preferred_element_type=jnp.float32)


def exchange(
    dens, mom, ene, wall, span, damp, damp_rows, fourth, order_in, order_out, shift,
    new_out, near, far,
    dy_out, dz_out, own, apart, lines_y, lines_z, dy_send, dz_send, wall_f, wall_h, wall_l, flux_h, flux_l, span_3,
    z1s, z1r, z2s, z2r, x1s, x1r, x2s, x2r, x3s, x3r, y1s, y1r, y2s, y2r, y3s, y3r, load_sem, keep_sem,
):
    gy = lax.axis_index("gy")
    gz = lax.axis_index("gz")
    z_lo, x = gy // 4, lax.rem(gy, 4)
    y, z_hi, core = gz // 4, lax.rem(gz // 2, 2), lax.rem(gz, 2)
    slot = y * 2 + core
    pair = ((1 - z_lo) * 4 + x, gz)
    relay = ((1 - z_lo) * 4 + x, y * 4 + (1 - z_hi) * 2 + core)
    x_of = [lax.rem(x + d, 4) for d in range(4)]
    x_peers = [(z_lo * 4 + other, gz) for other in x_of]
    slot_of = [lax.rem(slot + d, 8) for d in range(8)]
    y_peers = [(gy, (other // 2) * 4 + z_hi * 2 + lax.rem(other, 2)) for other in slot_of]
    far_gz = y * 4 + (1 - z_hi) * 2 + core
    near_row = PAD + gy * ROWS
    far_row = PAD + pair[0] * ROWS

    def send(src, dst, ssem, rsem, peer):
        return pltpu.make_async_remote_copy(src, dst, ssem, rsem, device_id=peer, device_id_type=MESH)

    loads = []
    for h in range(2):
        lanes = pl.ds(h * LANES, LANES)
        loads += [
            pltpu.make_async_copy(dens.at[:, lanes], own.at[h, 0], load_sem.at[3 * h]),
            pltpu.make_async_copy(mom.at[:, :, lanes], own.at[h, pl.ds(1, 3)], load_sem.at[3 * h + 1]),
            pltpu.make_async_copy(ene.at[:, lanes], own.at[h, 4], load_sem.at[3 * h + 2]),
        ]
    load_wall = pltpu.make_async_copy(wall.at[pl.ds(z_lo * HALF, HALF), :], wall_f, load_sem.at[6])
    for copy in loads:
        copy.start()
    load_wall.start()

    barrier = pltpu.get_barrier_semaphore()
    for peer in [pair, relay] + x_peers[1:] + y_peers[1:]:
        pl.semaphore_signal(barrier, inc=1, device_id=peer, device_id_type=MESH)

    z1, z2 = [], []
    for u in range(CHUNKS):
        for copies, source, target, ssem, rsem, peer in (
            (z1, apart, near, z1s, z1r, pair),
            (z2, near, far, z2s, z2r, relay),
        ):
            copies.append(
                [
                    send(source.at[u, pl.ds(2 * j, 2)], target.at[u, pl.ds(2 * j, 2)], ssem.at[u, j], rsem.at[u, j], peer)
                    for j in range(2)
                ]
            )
    x1, x2, x3, keeps = [], [], [], []
    for u in range(CHUNKS):
        for copies, source, row, ssem, rsem in ((x1, apart, near_row, x1s, x1r), (x2, near, far_row, x2s, x2r)):
            target = lines_y.at[u, :, pl.ds(row, ROWS), :]
            copies.append(
                [
                    send(source.at[u, x_of[d]], target, ssem.at[u, d - 1], rsem.at[u, d - 1], x_peers[d])
                    for d in range(1, 4)
                ]
            )
        x3.append(
            [
                send(dy_send.at[u, x_of[d]], dy_out.at[u, x], x3s.at[u, d - 1], x3r.at[u, d - 1], x_peers[d])
                for d in range(1, 4)
            ]
        )
        keeps.append(
            [
                pltpu.make_async_copy(apart.at[u, x], lines_y.at[u, :, pl.ds(near_row, ROWS), :], keep_sem.at[u, 0]),
                pltpu.make_async_copy(near.at[u, x], lines_y.at[u, :, pl.ds(far_row, ROWS), :], keep_sem.at[u, 1]),
                pltpu.make_async_copy(
                    apart.at[u, :, :, pl.ds(slot * HOLD, HOLD), :], lines_z.at[u, gz], keep_sem.at[u, 2]
                ),
                pltpu.make_async_copy(
                    far.at[u, :, :, pl.ds(slot * HOLD, HOLD), :], lines_z.at[u, far_gz], keep_sem.at[u, 3]
                ),
                pltpu.make_async_copy(dy_send.at[u, x], dy_out.at[u, x], keep_sem.at[u, 4]),
            ]
        )
    y1, y2, y3, keep_dz = [], [], [], []
    for u in range(CHUNKS):
        y1.append(
            [
                send(
                    apart.at[u, :, :, pl.ds(slot_of[d] * HOLD, HOLD), :], lines_z.at[u, gz],
                    y1s.at[u, d - 1], y1r.at[u, d - 1], y_peers[d],
                )
                for d in range(1, 8)
            ]
        )
        y2.append(
            [
                [
                    send(
                        far.at[u, pl.ds(2 * j, 2), :, pl.ds(slot_of[d] * HOLD, HOLD), :],
                        lines_z.at[u, far_gz, pl.ds(2 * j, 2)],
                        y2s.at[u, j, d - 1], y2r.at[u, j, d - 1], y_peers[d],
                    )
                    for d in range(1, 8)
                ]
                for j in range(2)
            ]
        )
    for h in range(2):
        home = dz_out.at[pl.ds(2 * h, 2), :, :, pl.ds(slot * HOLD, HOLD), :]
        y3.append(
            [
                send(dz_send.at[h, :, slot_of[d]], home, y3s.at[h, d - 1], y3r.at[h, d - 1], y_peers[d])
                for d in range(1, 8)
            ]
        )
        keep_dz.append(pltpu.make_async_copy(dz_send.at[h, :, slot], home, keep_sem.at[h, 5]))

    for copy in loads:
        copy.wait()
    for u in range(CHUNKS):
        h, e = u // 2, u % 2

        @pl.loop(0, 5)
        def _(f):
            for k in range(4):
                apart[u, k, f] = own[h, f, pl.ds(2 * k + e, ROWS, stride=PLANES), :]

        if u == 0:
            pl.semaphore_wait(barrier, 12)
        for copy in z1[u]:
            copy.start()
        for copy in x1[u]:
            copy.start()
        for copy in y1[u]:
            copy.start()
        keeps[u][0].start()
        keeps[u][2].start()

    load_wall.wait()

    @pl.loop(0, HALF // 64)
    def _(i):
        rows = pl.ds(i * 64, 64)
        high, low = split(wall_f[rows, :])
        wall_h[rows, :] = high
        wall_l[rows, :] = low

    high, low = [
        dot(order_out[z_hi], dot(part, order_in[...]).astype(jnp.bfloat16)).astype(jnp.bfloat16) for part in split(span[...])
    ]
    span_3[:, 0:NZ] = high
    span_3[:, NZ : 2 * NZ] = high
    span_3[:, 2 * NZ : 3 * NZ] = low
    for u in range(CHUNKS):
        for f in range(5):
            lines_y[u, f, 0:PAD, :] = jnp.zeros((PAD, LANES), jnp.float32)
            lines_y[u, f, PAD + NY : 2 * PAD + NY, :] = jnp.zeros((PAD, LANES), jnp.float32)

    @pl.loop(0, ROWS * PLANES // 64)
    def _(i):
        rows = pl.ds(i * 64, 64)
        c = [jnp.concatenate([own[0, f, rows, :], own[1, f, rows, :]], axis=1) for f in range(5)]
        for f, value in enumerate(flux_along(c, 0)):
            high, low = split(value)
            along = (dot(high, shift[...]) + dot(low, shift[...])) * (1.0 / 12.0)
            value = c[f] - TIME_STEP * along
            for h in range(2):
                own[h, f, rows, :] = value[:, h * LANES : (h + 1) * LANES]

    def pass_near(u, j):
        z1[u][j].wait_recv()
        z2[u][j].start()
        if j == 1:
            for copy in x2[u]:
                copy.start()
            keeps[u][1].start()

    def pass_far(u, j):
        z2[u][j].wait_recv()
        for copy in y2[u][j]:
            copy.start()
        if j == 1:
            keeps[u][3].start()

    def derive_y(u):
        keeps[u][0].wait()
        keeps[u][1].wait()
        for copy in x1[u] + x2[u]:
            copy.wait_recv()

        @pl.loop(0, NY // 64)
        def _(i):
            r = pl.multiple_of(i * 64, 64)
            c = [lines_y[u, f, pl.ds(PAD + r, 64), :] for f in range(5)]
            for f, value in enumerate(flux_along(c, 1)):
                high, low = split(value)
                flux_h[pl.ds(r, 64), f * LANES : (f + 1) * LANES] = high
                flux_l[pl.ds(r, 64), f * LANES : (f + 1) * LANES] = low

        @pl.loop(0, 4)
        def _(k):
            rows = pl.ds(pl.multiple_of(k * ROWS, ROWS), ROWS)
            total = dot(wall_h[rows, :], flux_h[...])
            total += dot(wall_h[rows, :], flux_l[...])
            total += dot(wall_l[rows, :], flux_h[...])
            block = z_lo * 4 + k
            weight = jnp.broadcast_to(damp_rows[pl.ds(block, 1), :], (ROWS, LANES)).T
            for f in range(5):
                window = lines_y[u, f, pl.ds(pl.multiple_of(block * ROWS, ROWS), ROWS + 2 * PAD), :]

                def at(step, window=window):
                    return window[PAD + step : PAD + step + ROWS]

                smooth = at(-2) - 4.0 * at(-1) + 6.0 * at(0) - 4.0 * at(1) + at(2)
                dy_send[u, k, f] = total[:, f * LANES : (f + 1) * LANES] + weight * smooth

        for copy in x3[u]:
            copy.start()
        keeps[u][4].start()

    def derive_z(h):
        for u in (2 * h, 2 * h + 1):
            keeps[u][2].wait()
            keeps[u][3].wait()
            for copy in y1[u] + y2[u][0] + y2[u][1]:
                copy.wait_recv()
        lines = lines_z.reshape(CHUNKS, GZ * 4 * 5 * HOLD, LANES)
        results = dz_send.reshape(2, 2 * 8 * 4 * 5 * HOLD, LANES)

        @pl.loop(0, HOLD)
        def _(r):
            weight = damp[gy * ROWS + slot * HOLD + r]
            c = []
            for f in range(5):
                at = pl.ds(f * HOLD + r, NZ // 2, stride=5 * HOLD)
                c.append(jnp.concatenate([lines[2 * h, at, :], lines[2 * h + 1, at, :]], axis=0))
            high, low = split(jnp.concatenate(flux_along(c, 2), axis=1))
            total = dot(span_3[...], jnp.concatenate([high, low, high], axis=0))
            high, low = split(jnp.concatenate(c, axis=1))
            total += weight * dot(fourth[z_hi], jnp.concatenate([high, low], axis=0))
            for f in range(5):
                at = pl.ds(f * HOLD + r, NZ // 2, stride=5 * HOLD)
                results[h, at, :] = total[:, f * LANES : (f + 1) * LANES]

        for copy in y3[h]:
            copy.start()
        keep_dz[h].start()

    def add(h, source):
        @pl.loop(0, 5)
        def _(f):
            for e in range(2):
                for k in range(4):
                    at = pl.ds(2 * k + e, ROWS, stride=PLANES)
                    own[h, f, at, :] = own[h, f, at, :] - TIME_STEP * source[2 * h + e, k, f]

    def add_y(h):
        for u in (2 * h, 2 * h + 1):
            keeps[u][4].wait()
            for copy in x3[u]:
                copy.wait_recv()
        add(h, dy_out)

    saves = [pltpu.make_async_copy(own.at[h], new_out.at[h], load_sem.at[h]) for h in range(2)]

    def add_z(h):
        keep_dz[h].wait()
        for copy in y3[h]:
            copy.wait_recv()
        add(h, dz_out)
        saves[h].start()

    pass_near(0, 0)
    pass_near(0, 1)
    pass_far(0, 0)
    pass_near(1, 0)
    pass_far(0, 1)
    pass_near(1, 1)
    pass_far(1, 0)
    pass_near(2, 0)
    pass_far(1, 1)
    derive_y(0)
    pass_near(2, 1)
    pass_far(2, 0)
    derive_z(0)
    derive_y(1)
    pass_near(3, 0)
    pass_far(2, 1)
    pass_near(3, 1)
    pass_far(3, 0)
    derive_y(2)
    pass_far(3, 1)
    derive_z(1)
    derive_y(3)
    add_y(0)
    add_z(0)
    add_y(1)
    add_z(1)

    for h in range(2):
        saves[h].wait()
        for copy in y3[h]:
            copy.wait_send()
    for u in range(CHUNKS):
        for copy in z1[u] + z2[u] + x1[u] + x2[u] + x3[u] + y1[u] + y2[u][0] + y2[u][1]:
            copy.wait_send()


def join(halves, new_dens, new_mom, new_ene, whole, in_sem, out_sem):
    targets = [new_dens, new_mom.at[0], new_mom.at[1], new_mom.at[2], new_ene]
    ins = [
        [
            pltpu.make_async_copy(halves.at[h, f], whole.at[f, :, pl.ds(h * LANES, LANES)], in_sem.at[f, h])
            for h in range(2)
        ]
        for f in range(5)
    ]
    outs = [pltpu.make_async_copy(whole.at[f], targets[f], out_sem.at[f]) for f in range(5)]
    for f in range(5):
        for copy in ins[f]:
            copy.start()
    for f in range(5):
        for copy in ins[f]:
            copy.wait()
        outs[f].start()
    for copy in outs:
        copy.wait()


def plane_order():
    return np.arange(NZ).reshape(GZ, 4, 2).transpose(2, 0, 1).reshape(-1)


def half_order(z_hi):
    return np.arange(NZ).reshape(4, 2, 2, 4, 2)[:, z_hi].transpose(3, 0, 1, 2).reshape(-1)


def order_matrices():
    eye = np.eye(NZ, dtype=np.float32)
    return eye[:, plane_order()], np.stack([eye[half_order(z)] for z in range(2)])


def fourth_matrix():
    m = np.zeros((NZ, NZ), np.float32)
    for i in range(NZ):
        for k, w in ((-2, 1.0), (-1, -4.0), (0, 6.0), (1, -4.0), (2, 1.0)):
            m[i, (i + k) % NZ] += w
    m = np.stack([m[half_order(z)][:, plane_order()] for z in range(2)])
    return np.concatenate([m, m], axis=2)


def shift_matrix():
    m = np.zeros((CELLS, CELLS), np.float32)
    for i in range(CELLS):
        for k, w in ((1, 8.0), (-1, -8.0), (2, -1.0), (-2, 1.0)):
            m[min(max(i + k, 0), CELLS - 1), i] += w
    return m


ANY = pl.BlockSpec(memory_space=pl.ANY)
VMEM = pl.BlockSpec(memory_space=pltpu.VMEM)
SMEM = pl.BlockSpec(memory_space=pltpu.SMEM)
DMA = pltpu.SemaphoreType.DMA


def local(density, momentum, energy, wall_operator, span_operator, damping):
    cells = ROWS * PLANES
    dens = density.reshape(cells, CELLS)
    mom = momentum.reshape(3, cells, CELLS)
    ene = energy.reshape(cells, CELLS)
    f32, bf16 = jnp.float32, jnp.bfloat16
    order_in, order_out = order_matrices()
    whole = jax.ShapeDtypeStruct((CHUNKS, 4, 5, ROWS, LANES), f32)
    halves, _, _ = pl.pallas_call(
        exchange,
        out_shape=(jax.ShapeDtypeStruct((2, 5, cells, LANES), f32), whole, whole),
        in_specs=[ANY, ANY, ANY, ANY, VMEM, SMEM, VMEM, VMEM, VMEM, VMEM, VMEM],
        out_specs=(ANY,) * 3,
        scratch_shapes=[
            pltpu.VMEM((CHUNKS, 4, 5, ROWS, LANES), f32),
            pltpu.VMEM((CHUNKS, 4, 5, ROWS, LANES), f32),
            pltpu.VMEM((2, 5, cells, LANES), f32),
            pltpu.VMEM((CHUNKS, 4, 5, ROWS, LANES), f32),
            pltpu.VMEM((CHUNKS, 5, NY + 2 * PAD, LANES), f32),
            pltpu.VMEM((CHUNKS, GZ, 4, 5, HOLD, LANES), f32),
            pltpu.VMEM((CHUNKS, 4, 5, ROWS, LANES), f32),
            pltpu.VMEM((2, 2, 8, 4, 5, HOLD, LANES), f32),
            pltpu.VMEM((HALF, NY), f32),
            pltpu.VMEM((HALF, NY), bf16),
            pltpu.VMEM((HALF, NY), bf16),
            pltpu.VMEM((NY, 5 * LANES), bf16),
            pltpu.VMEM((NY, 5 * LANES), bf16),
            pltpu.VMEM((NZ // 2, 3 * NZ), bf16),
            *[DMA((CHUNKS, 2))] * 4,
            *[DMA((CHUNKS, 3))] * 6,
            *[DMA((CHUNKS, 7))] * 2,
            *[DMA((CHUNKS, 2, 7))] * 2,
            *[DMA((2, 7))] * 2,
            DMA((7,)),
            DMA((CHUNKS, 6)),
        ],
        compiler_params=pltpu.CompilerParams(
            collective_id=0, has_side_effects=True, vmem_limit_bytes=62 << 20
        ),
        name="exchange",
    )(
        dens, mom, ene, wall_operator, span_operator, damping, damping.reshape(GY, ROWS),
        jnp.asarray(fourth_matrix(), bf16), jnp.asarray(order_in, bf16), jnp.asarray(order_out, bf16),
        jnp.asarray(shift_matrix(), bf16),
    )
    new = pl.pallas_call(
        join,
        out_shape=(
            jax.ShapeDtypeStruct((cells, CELLS), f32),
            jax.ShapeDtypeStruct((3, cells, CELLS), f32),
            jax.ShapeDtypeStruct((cells, CELLS), f32),
        ),
        in_specs=[ANY],
        out_specs=(ANY,) * 3,
        scratch_shapes=[pltpu.VMEM((5, cells, CELLS), f32), DMA((5, 2)), DMA((5,))],
        name="join",
    )(halves)
    shape = (ROWS, PLANES, CELLS)
    return new[0].reshape(shape), new[1].reshape((3,) + shape), new[2].reshape(shape)


def solution(mesh):
    in_specs = (P("gy", "gz", None), P(None, "gy", "gz", None), P("gy", "gz", None), P(), P(), P())
    out_specs = (P("gy", "gz", None), P(None, "gy", "gz", None), P("gy", "gz", None))
    return jax.shard_map(local, mesh=mesh, in_specs=in_specs, out_specs=out_specs, check_vma=False)
```

```python
import functools

import jax
import jax.numpy as jnp
import numpy as np
from jax import lax
from jax.experimental import pallas as pl
from jax.experimental.pallas import tpu as pltpu
from jax.sharding import PartitionSpec as P

MESH = pl.DeviceIdType.MESH
GAMMA_LESS = 0.4
TIME_STEP = 0.1
GY, GZ = 8, 16
ROWS, PLANES, CELLS, LANES = 128, 8, 256, 128
NY, NZ = GY * ROWS, GZ * PLANES
HOLD = 16
CHUNKS = 4
HALF = NY // 2
GROUPS = ROWS // HOLD


def flux_along(c, direction):
    inverse = 1.0 / c[0]
    velocity = c[1 + direction] * inverse
    kinetic = 0.5 * (c[1] * c[1] + c[2] * c[2] + c[3] * c[3]) * inverse
    pressure = GAMMA_LESS * (c[4] - kinetic)
    out = [c[1 + direction]]
    for column in range(3):
        product = c[1 + column] * velocity
        if column == direction:
            product = product + pressure
        out.append(product)
    out.append((c[4] + pressure) * velocity)
    return out


def split(x):
    high = x.astype(jnp.bfloat16)
    low = (x - high.astype(jnp.float32)).astype(jnp.bfloat16)
    return high, low


def dot(a, b):
    return jnp.dot(a, b, preferred_element_type=jnp.float32)


def exchange(
    dens, mom, ene, wall, span, damp, damp_rows, fourth, order_in, order_out, shift,
    new_out, near, far,
    dy_out, dz_out, own, apart, lines_y, lines_z, dy_send, dz_send, wall_f, wall_h, wall_l, flux_h, flux_l, span_2,
    z1s, z1r, z2s, z2r, x1s, x1r, x2s, x2r, x3s, x3r, y1s, y1r, y2s, y2r, y3s, y3r, load_sem, keep_sem, save_sem,
):
    gy = lax.axis_index("gy")
    gz = lax.axis_index("gz")
    z_lo, x = gy // 4, lax.rem(gy, 4)
    y, z_hi, core = gz // 4, lax.rem(gz // 2, 2), lax.rem(gz, 2)
    slot = y * 2 + core
    pair = ((1 - z_lo) * 4 + x, gz)
    relay = ((1 - z_lo) * 4 + x, y * 4 + (1 - z_hi) * 2 + core)
    x_of = [lax.rem(x + d, 4) for d in range(4)]
    x_peers = [(z_lo * 4 + other, gz) for other in x_of]
    slot_of = [lax.rem(slot + d, 8) for d in range(8)]
    y_peers = [(gy, (other // 2) * 4 + z_hi * 2 + lax.rem(other, 2)) for other in slot_of]
    far_gz = y * 4 + (1 - z_hi) * 2 + core
    near_group = 1 + gy * GROUPS
    far_group = 1 + pair[0] * GROUPS

    def send(src, dst, ssem, rsem, peer):
        return pltpu.make_async_remote_copy(src, dst, ssem, rsem, device_id=peer, device_id_type=MESH)

    loads = []
    for h in range(2):
        lanes = pl.ds(h * LANES, LANES)
        loads += [
            pltpu.make_async_copy(dens.at[:, lanes], own.at[h, 0], load_sem.at[3 * h]),
            pltpu.make_async_copy(mom.at[:, :, lanes], own.at[h, pl.ds(1, 3)], load_sem.at[3 * h + 1]),
            pltpu.make_async_copy(ene.at[:, lanes], own.at[h, 4], load_sem.at[3 * h + 2]),
        ]
    load_wall = pltpu.make_async_copy(wall.at[pl.ds(z_lo * HALF, HALF), :], wall_f, load_sem.at[6])
    for copy in loads:
        copy.start()

    barrier = pltpu.get_barrier_semaphore()
    for peer in [pair, relay] + x_peers[1:] + y_peers[1:]:
        pl.semaphore_signal(barrier, inc=1, device_id=peer, device_id_type=MESH)

    z1, z2 = [], []
    for u in range(CHUNKS):
        for copies, source, target, ssem, rsem, peer in (
            (z1, apart, near, z1s, z1r, pair),
            (z2, near, far, z2s, z2r, relay),
        ):
            copies.append(
                [
                    send(source.at[u, :, pl.ds(2 * j, 2)], target.at[u, :, pl.ds(2 * j, 2)], ssem.at[u, j], rsem.at[u, j], peer)
                    for j in range(2)
                ]
            )
    x1, x2, x3, keeps = [], [], [], []
    for u in range(CHUNKS):
        for copies, source, group, ssem, rsem in ((x1, apart, near_group, x1s, x1r), (x2, near, far_group, x2s, x2r)):
            target = lines_y.at[u, pl.ds(group, GROUPS)]
            copies.append(
                [
                    send(source.at[u, :, x_of[d]], target, ssem.at[u, d - 1], rsem.at[u, d - 1], x_peers[d])
                    for d in range(1, 4)
                ]
            )
        x3.append(
            [
                send(dy_send.at[u, x_of[d]], dy_out.at[u, x], x3s.at[u, d - 1], x3r.at[u, d - 1], x_peers[d])
                for d in range(1, 4)
            ]
        )
        keeps.append(
            [
                pltpu.make_async_copy(apart.at[u, :, x], lines_y.at[u, pl.ds(near_group, GROUPS)], keep_sem.at[u, 0]),
                pltpu.make_async_copy(near.at[u, :, x], lines_y.at[u, pl.ds(far_group, GROUPS)], keep_sem.at[u, 1]),
                pltpu.make_async_copy(
                    apart.at[u, slot], lines_z.at[u, gz], keep_sem.at[u, 2]
                ),
                pltpu.make_async_copy(
                    far.at[u, slot], lines_z.at[u, far_gz], keep_sem.at[u, 3]
                ),
                pltpu.make_async_copy(dy_send.at[u, x], dy_out.at[u, x], keep_sem.at[u, 4]),
            ]
        )
    y1, y2, y3, keep_dz = [], [], [], []
    for u in range(CHUNKS):
        y1.append(
            [
                send(
                    apart.at[u, slot_of[d]], lines_z.at[u, gz],
                    y1s.at[u, d - 1], y1r.at[u, d - 1], y_peers[d],
                )
                for d in range(1, 8)
            ]
        )
        y2.append(
            [
                [
                    send(
                        far.at[u, slot_of[d], pl.ds(2 * j, 2)],
                        lines_z.at[u, far_gz, pl.ds(2 * j, 2)],
                        y2s.at[u, j, d - 1], y2r.at[u, j, d - 1], y_peers[d],
                    )
                    for d in range(1, 8)
                ]
                for j in range(2)
            ]
        )
    for h in range(2):
        home = dz_out.at[pl.ds(2 * h, 2), slot]
        y3.append(
            [
                [
                    send(
                        dz_send.at[h, :, slot_of[d], :, :, pl.ds(8 * part, 8), :],
                        dz_out.at[pl.ds(2 * h, 2), slot, :, :, pl.ds(8 * part, 8), :],
                        y3s.at[h, part, d - 1], y3r.at[h, part, d - 1], y_peers[d],
                    )
                    for d in range(1, 8)
                ]
                for part in range(2)
            ]
        )
        keep_dz.append(pltpu.make_async_copy(dz_send.at[h, :, slot], home, keep_sem.at[h, 5]))

    for u in range(CHUNKS):
        h, e = u // 2, u % 2
        if e == 0:
            for copy in loads[3 * h : 3 * h + 3]:
                copy.wait()

        @pl.loop(0, 5)
        def _(f):
            for k in range(4):
                planes = own[h, f, pl.ds(2 * k + e, ROWS, stride=PLANES), :]
                apart[u, :, k, f] = planes.reshape(GROUPS, HOLD, LANES)

        if u == 0:
            pl.semaphore_wait(barrier, 12)
        for copy in z1[u]:
            copy.start()
        for copy in x1[u]:
            copy.start()
        for copy in y1[u]:
            copy.start()
        keeps[u][0].start()
        keeps[u][2].start()

    load_wall.start()

    load_wall.wait()

    @pl.loop(0, HALF // 64)
    def _(i):
        rows = pl.ds(i * 64, 64)
        high, low = split(wall_f[rows, :])
        wall_h[rows, :] = high
        wall_l[rows, :] = low

    high, low = [
        dot(order_out[z_hi], dot(part, order_in[...]).astype(jnp.bfloat16)).astype(jnp.bfloat16) for part in split(span[...])
    ]
    span_2[0 : NZ // 2, 0:NZ] = high
    span_2[0 : NZ // 2, NZ : 2 * NZ] = high
    span_2[NZ // 2 : NZ, 0:NZ] = low
    span_2[NZ // 2 : NZ, NZ : 2 * NZ] = jnp.zeros((NZ // 2, NZ), jnp.bfloat16)
    for u in range(CHUNKS):
        for f in range(5):
            for group in (0, NY // HOLD + 1):
                lines_y[u, group, f] = jnp.zeros((HOLD, LANES), jnp.float32)

    @pl.loop(0, ROWS * PLANES // 64)
    def _(i):
        rows = pl.ds(i * 64, 64)
        c = [jnp.concatenate([own[0, f, rows, :], own[1, f, rows, :]], axis=1) for f in range(5)]
        for f, value in enumerate(flux_along(c, 0)):
            high, low = split(value)
            along = (dot(high, shift[...]) + dot(low, shift[...])) * (1.0 / 12.0)
            value = c[f] - TIME_STEP * along
            for h in range(2):
                own[h, f, rows, :] = value[:, h * LANES : (h + 1) * LANES]

    def pass_near(u, j):
        z1[u][j].wait_recv()
        z2[u][j].start()
        if j == 1:
            for copy in x2[u]:
                copy.start()
            keeps[u][1].start()

    def pass_far(u, j):
        z2[u][j].wait_recv()
        for copy in y2[u][j]:
            copy.start()
        if j == 1:
            keeps[u][3].start()

    def derive_y(u):
        keeps[u][0].wait()
        keeps[u][1].wait()
        for copy in x1[u] + x2[u]:
            copy.wait_recv()

        @pl.loop(0, NY // 64)
        def _(i):
            r = pl.multiple_of(i * 64, 64)
            c = [lines_y[u, pl.ds(1 + i * 4, 4), f].reshape(64, LANES) for f in range(5)]
            for f, value in enumerate(flux_along(c, 1)):
                high, low = split(value)
                flux_h[pl.ds(r, 64), f * LANES : (f + 1) * LANES] = high
                flux_l[pl.ds(r, 64), f * LANES : (f + 1) * LANES] = low

        @pl.loop(0, 4)
        def _(k):
            rows = pl.ds(pl.multiple_of(k * ROWS, ROWS), ROWS)
            total = dot(wall_h[rows, :], flux_h[...])
            total += dot(wall_h[rows, :], flux_l[...])
            total += dot(wall_l[rows, :], flux_h[...])
            block = z_lo * 4 + k
            weight = jnp.broadcast_to(damp_rows[pl.ds(block, 1), :], (ROWS, LANES)).T
            for f in range(5):
                window = lines_y[u, pl.ds(block * GROUPS, GROUPS + 2), f].reshape(ROWS + 2 * HOLD, LANES)

                def at(step, window=window):
                    return window[HOLD + step : HOLD + step + ROWS]

                smooth = at(-2) - 4.0 * at(-1) + 6.0 * at(0) - 4.0 * at(1) + at(2)
                total_f = total[:, f * LANES : (f + 1) * LANES] + weight * smooth
                dy_send[u, k, :, f] = total_f.reshape(GROUPS, HOLD, LANES)

        for copy in x3[u]:
            copy.start()
        keeps[u][4].start()

    def derive_z(h):
        for u in (2 * h, 2 * h + 1):
            keeps[u][2].wait()
            keeps[u][3].wait()
            for copy in y1[u] + y2[u][0] + y2[u][1]:
                copy.wait_recv()
        lines = lines_z.reshape(CHUNKS, GZ * 4 * 5 * HOLD, LANES)
        results = dz_send.reshape(2, 2 * 8 * 4 * 5 * HOLD, LANES)

        for part in range(2):

            @pl.loop(8 * part, 8 * part + 8)
            def _(r):
                weight = damp[gy * ROWS + slot * HOLD + r]
                c = []
                for f in range(5):
                    at = pl.ds(f * HOLD + r, NZ // 2, stride=5 * HOLD)
                    c.append(jnp.concatenate([lines[2 * h, at, :], lines[2 * h + 1, at, :]], axis=0))
                high, low = split(jnp.concatenate(flux_along(c, 2), axis=1))
                both = dot(span_2[...], jnp.concatenate([high, low], axis=0))
                high, low = split(jnp.concatenate(c, axis=1))
                total = weight * dot(fourth[z_hi], jnp.concatenate([high, low], axis=0))
                total += both[0 : NZ // 2] + both[NZ // 2 :]
                for f in range(5):
                    at = pl.ds(f * HOLD + r, NZ // 2, stride=5 * HOLD)
                    results[h, at, :] = total[:, f * LANES : (f + 1) * LANES]

            for copy in y3[h][part]:
                copy.start()
        keep_dz[h].start()

    def add(h, f, source):
        for e in range(2):
            for k in range(4):
                at = pl.ds(2 * k + e, ROWS, stride=PLANES)
                part = source(2 * h + e, k).reshape(ROWS, LANES)
                own[h, f, at, :] = own[h, f, at, :] - TIME_STEP * part

    def add_y(h):
        for u in (2 * h, 2 * h + 1):
            keeps[u][4].wait()
            for copy in x3[u]:
                copy.wait_recv()

        @pl.loop(0, 5)
        def _(f):
            add(h, f, lambda u, k: dy_out[u, k, :, f])

    saves = [
        [pltpu.make_async_copy(own.at[h, f], new_out.at[h, f], save_sem.at[h, f]) for f in range(5)] for h in range(2)
    ]

    def add_z(h):
        keep_dz[h].wait()
        for copy in y3[h][0] + y3[h][1]:
            copy.wait_recv()
        for f in range(5):
            add(h, f, lambda u, k, f=f: dz_out[u, :, k, f])
            saves[h][f].start()

    pass_near(0, 0)
    pass_near(0, 1)
    pass_far(0, 0)
    pass_near(1, 0)
    pass_far(0, 1)
    pass_near(1, 1)
    pass_far(1, 0)
    pass_near(2, 0)
    pass_far(1, 1)
    derive_y(0)
    pass_near(2, 1)
    pass_far(2, 0)
    derive_z(0)
    derive_y(1)
    pass_near(3, 0)
    pass_far(2, 1)
    pass_near(3, 1)
    pass_far(3, 0)
    derive_y(2)
    pass_far(3, 1)
    derive_z(1)
    derive_y(3)
    add_y(0)
    add_z(0)
    add_y(1)
    add_z(1)

    for h in range(2):
        for copy in y3[h][0] + y3[h][1]:
            copy.wait_send()
    for u in range(CHUNKS):
        for copy in z1[u] + z2[u] + x1[u] + x2[u] + x3[u] + y1[u] + y2[u][0] + y2[u][1]:
            copy.wait_send()
    for copy in saves[0] + saves[1]:
        copy.wait()


def join(halves, new_dens, new_mom, new_ene, whole, in_sem, out_sem):
    targets = [new_dens, new_mom.at[0], new_mom.at[1], new_mom.at[2], new_ene]
    ins = [
        [
            pltpu.make_async_copy(halves.at[h, f], whole.at[f, :, pl.ds(h * LANES, LANES)], in_sem.at[f, h])
            for h in range(2)
        ]
        for f in range(5)
    ]
    outs = [pltpu.make_async_copy(whole.at[f], targets[f], out_sem.at[f]) for f in range(5)]
    for f in range(5):
        for copy in ins[f]:
            copy.start()
    for f in range(5):
        for copy in ins[f]:
            copy.wait()
        outs[f].start()
    for copy in outs:
        copy.wait()


def plane_order():
    return np.arange(NZ).reshape(GZ, 4, 2).transpose(2, 0, 1).reshape(-1)


def half_order(z_hi):
    return np.arange(NZ).reshape(4, 2, 2, 4, 2)[:, z_hi].transpose(3, 0, 1, 2).reshape(-1)


def order_matrices():
    eye = np.eye(NZ, dtype=np.float32)
    return eye[:, plane_order()], np.stack([eye[half_order(z)] for z in range(2)])


def fourth_matrix():
    m = np.zeros((NZ, NZ), np.float32)
    for i in range(NZ):
        for k, w in ((-2, 1.0), (-1, -4.0), (0, 6.0), (1, -4.0), (2, 1.0)):
            m[i, (i + k) % NZ] += w
    m = np.stack([m[half_order(z)][:, plane_order()] for z in range(2)])
    return np.concatenate([m, m], axis=2)


def shift_matrix():
    m = np.zeros((CELLS, CELLS), np.float32)
    for i in range(CELLS):
        for k, w in ((1, 8.0), (-1, -8.0), (2, -1.0), (-2, 1.0)):
            m[min(max(i + k, 0), CELLS - 1), i] += w
    return m


ANY = pl.BlockSpec(memory_space=pl.ANY)
VMEM = pl.BlockSpec(memory_space=pltpu.VMEM)
SMEM = pl.BlockSpec(memory_space=pltpu.SMEM)
DMA = pltpu.SemaphoreType.DMA


def local(density, momentum, energy, wall_operator, span_operator, damping):
    cells = ROWS * PLANES
    dens = density.reshape(cells, CELLS)
    mom = momentum.reshape(3, cells, CELLS)
    ene = energy.reshape(cells, CELLS)
    f32, bf16 = jnp.float32, jnp.bfloat16
    order_in, order_out = order_matrices()
    whole = jax.ShapeDtypeStruct((CHUNKS, GROUPS, 4, 5, HOLD, LANES), f32)
    halves, _, _ = pl.pallas_call(
        exchange,
        out_shape=(jax.ShapeDtypeStruct((2, 5, cells, LANES), f32), whole, whole),
        in_specs=[ANY, ANY, ANY, ANY, VMEM, SMEM, VMEM, VMEM, VMEM, VMEM, VMEM],
        out_specs=(ANY,) * 3,
        scratch_shapes=[
            pltpu.VMEM((CHUNKS, 4, GROUPS, 5, HOLD, LANES), f32),
            pltpu.VMEM((CHUNKS, GROUPS, 4, 5, HOLD, LANES), f32),
            pltpu.VMEM((2, 5, cells, LANES), f32),
            pltpu.VMEM((CHUNKS, GROUPS, 4, 5, HOLD, LANES), f32),
            pltpu.VMEM((CHUNKS, NY // HOLD + 2, 5, HOLD, LANES), f32),
            pltpu.VMEM((CHUNKS, GZ, 4, 5, HOLD, LANES), f32),
            pltpu.VMEM((CHUNKS, 4, GROUPS, 5, HOLD, LANES), f32),
            pltpu.VMEM((2, 2, 8, 4, 5, HOLD, LANES), f32),
            pltpu.VMEM((HALF, NY), f32),
            pltpu.VMEM((HALF, NY), bf16),
            pltpu.VMEM((HALF, NY), bf16),
            pltpu.VMEM((NY, 5 * LANES), bf16),
            pltpu.VMEM((NY, 5 * LANES), bf16),
            pltpu.VMEM((NZ, 2 * NZ), bf16),
            *[DMA((CHUNKS, 2))] * 4,
            *[DMA((CHUNKS, 3))] * 6,
            *[DMA((CHUNKS, 7))] * 2,
            *[DMA((CHUNKS, 2, 7))] * 2,
            *[DMA((2, 2, 7))] * 2,
            DMA((7,)),
            DMA((CHUNKS, 6)),
            DMA((2, 5)),
        ],
        compiler_params=pltpu.CompilerParams(
            collective_id=0, has_side_effects=True, vmem_limit_bytes=62 << 20
        ),
        name="exchange",
    )(
        dens, mom, ene, wall_operator, span_operator, damping, damping.reshape(GY, ROWS),
        jnp.asarray(fourth_matrix(), bf16), jnp.asarray(order_in, bf16), jnp.asarray(order_out, bf16),
        jnp.asarray(shift_matrix(), bf16),
    )
    new = pl.pallas_call(
        join,
        out_shape=(
            jax.ShapeDtypeStruct((cells, CELLS), f32),
            jax.ShapeDtypeStruct((3, cells, CELLS), f32),
            jax.ShapeDtypeStruct((cells, CELLS), f32),
        ),
        in_specs=[ANY],
        out_specs=(ANY,) * 3,
        scratch_shapes=[pltpu.VMEM((5, cells, CELLS), f32), DMA((5, 2)), DMA((5,))],
        name="join",
    )(halves)
    shape = (ROWS, PLANES, CELLS)
    return new[0].reshape(shape), new[1].reshape((3,) + shape), new[2].reshape(shape)


def solution(mesh):
    in_specs = (P("gy", "gz", None), P(None, "gy", "gz", None), P("gy", "gz", None), P(), P(), P())
    out_specs = (P("gy", "gz", None), P(None, "gy", "gz", None), P("gy", "gz", None))
    return jax.shard_map(local, mesh=mesh, in_specs=in_specs, out_specs=out_specs, check_vma=False)
```

```python
import functools

import jax
import jax.numpy as jnp
import numpy as np
from jax import lax
from jax.experimental import pallas as pl
from jax.experimental.pallas import tpu as pltpu
from jax.sharding import PartitionSpec as P

MESH = pl.DeviceIdType.MESH
GAMMA_LESS = 0.4
TIME_STEP = 0.1
GY, GZ = 8, 16
ROWS, PLANES, CELLS, LANES = 128, 8, 256, 128
NY, NZ = GY * ROWS, GZ * PLANES
HOLD = 16
CHUNKS = 4
HALF = NY // 2
GROUPS = ROWS // HOLD


def flux_along(c, direction):
    inverse = 1.0 / c[0]
    velocity = c[1 + direction] * inverse
    kinetic = 0.5 * (c[1] * c[1] + c[2] * c[2] + c[3] * c[3]) * inverse
    pressure = GAMMA_LESS * (c[4] - kinetic)
    out = [c[1 + direction]]
    for column in range(3):
        product = c[1 + column] * velocity
        if column == direction:
            product = product + pressure
        out.append(product)
    out.append((c[4] + pressure) * velocity)
    return out


def split(x):
    high = x.astype(jnp.bfloat16)
    low = (x - high.astype(jnp.float32)).astype(jnp.bfloat16)
    return high, low


def dot(a, b):
    return jnp.dot(a, b, preferred_element_type=jnp.float32)


def exchange(
    dens, mom, ene, wall, span, damp, damp_rows, fourth, order_in, order_out, shift,
    new_out, near, far,
    dy_out, dz_out, own, apart, lines_y, lines_z, dy_send, dz_send, wall_f, wall_h, wall_l, flux_h, flux_l, span_2,
    z1s, z1r, z2s, z2r, x1s, x1r, x2s, x2r, x3s, x3r, y1s, y1r, y2s, y2r, y3s, y3r, load_sem, keep_sem, save_sem,
):
    gy = lax.axis_index("gy")
    gz = lax.axis_index("gz")
    z_lo, x = gy // 4, lax.rem(gy, 4)
    y, z_hi, core = gz // 4, lax.rem(gz // 2, 2), lax.rem(gz, 2)
    slot = y * 2 + core
    pair = ((1 - z_lo) * 4 + x, gz)
    relay = ((1 - z_lo) * 4 + x, y * 4 + (1 - z_hi) * 2 + core)
    x_of = [lax.rem(x + d, 4) for d in range(4)]
    x_peers = [(z_lo * 4 + other, gz) for other in x_of]
    slot_of = [lax.rem(slot + d, 8) for d in range(8)]
    y_peers = [(gy, (other // 2) * 4 + z_hi * 2 + lax.rem(other, 2)) for other in slot_of]
    far_gz = y * 4 + (1 - z_hi) * 2 + core
    near_group = 1 + gy * GROUPS
    far_group = 1 + pair[0] * GROUPS

    def send(src, dst, ssem, rsem, peer):
        return pltpu.make_async_remote_copy(src, dst, ssem, rsem, device_id=peer, device_id_type=MESH)

    loads = []
    for h in range(2):
        lanes = pl.ds(h * LANES, LANES)
        loads += [
            pltpu.make_async_copy(dens.at[:, lanes], own.at[h, 0], load_sem.at[3 * h]),
            pltpu.make_async_copy(mom.at[:, :, lanes], own.at[h, pl.ds(1, 3)], load_sem.at[3 * h + 1]),
            pltpu.make_async_copy(ene.at[:, lanes], own.at[h, 4], load_sem.at[3 * h + 2]),
        ]
    load_wall = pltpu.make_async_copy(wall.at[pl.ds(z_lo * HALF, HALF), :], wall_f, load_sem.at[6])
    for copy in loads:
        copy.start()

    barrier = pltpu.get_barrier_semaphore()
    for peer in [pair, relay] + x_peers[1:] + y_peers[1:]:
        pl.semaphore_signal(barrier, inc=1, device_id=peer, device_id_type=MESH)

    z1, z2 = [], []
    for u in range(CHUNKS):
        for copies, source, target, ssem, rsem, peer in (
            (z1, apart, near, z1s, z1r, pair),
            (z2, near, far, z2s, z2r, relay),
        ):
            copies.append(
                [
                    send(source.at[u, :, pl.ds(2 * j, 2)], target.at[u, :, pl.ds(2 * j, 2)], ssem.at[u, j], rsem.at[u, j], peer)
                    for j in range(2)
                ]
            )
    x1, x2, x3, keeps = [], [], [], []
    for u in range(CHUNKS):
        for copies, source, group, ssem, rsem in ((x1, apart, near_group, x1s, x1r), (x2, near, far_group, x2s, x2r)):
            target = lines_y.at[u, pl.ds(group, GROUPS)]
            copies.append(
                [
                    send(source.at[u, :, x_of[d]], target, ssem.at[u, d - 1], rsem.at[u, d - 1], x_peers[d])
                    for d in range(1, 4)
                ]
            )
        x3.append(
            [
                send(dy_send.at[u, x_of[d]], dy_out.at[u, x], x3s.at[u, d - 1], x3r.at[u, d - 1], x_peers[d])
                for d in range(1, 4)
            ]
        )
        keeps.append(
            [
                pltpu.make_async_copy(apart.at[u, :, x], lines_y.at[u, pl.ds(near_group, GROUPS)], keep_sem.at[u, 0]),
                pltpu.make_async_copy(near.at[u, :, x], lines_y.at[u, pl.ds(far_group, GROUPS)], keep_sem.at[u, 1]),
                pltpu.make_async_copy(
                    apart.at[u, slot], lines_z.at[u, gz], keep_sem.at[u, 2]
                ),
                pltpu.make_async_copy(
                    far.at[u, slot], lines_z.at[u, far_gz], keep_sem.at[u, 3]
                ),
                pltpu.make_async_copy(dy_send.at[u, x], dy_out.at[u, x], keep_sem.at[u, 4]),
            ]
        )
    y1, y2, y3, keep_dz = [], [], [], []
    for u in range(CHUNKS):
        y1.append(
            [
                send(
                    apart.at[u, slot_of[d]], lines_z.at[u, gz],
                    y1s.at[u, d - 1], y1r.at[u, d - 1], y_peers[d],
                )
                for d in range(1, 8)
            ]
        )
        y2.append(
            [
                [
                    send(
                        far.at[u, slot_of[d], pl.ds(2 * j, 2)],
                        lines_z.at[u, far_gz, pl.ds(2 * j, 2)],
                        y2s.at[u, j, d - 1], y2r.at[u, j, d - 1], y_peers[d],
                    )
                    for d in range(1, 8)
                ]
                for j in range(2)
            ]
        )
    for h in range(2):
        home = dz_out.at[pl.ds(2 * h, 2), slot]
        y3.append(
            [
                [
                    send(
                        dz_send.at[h, :, slot_of[d], :, :, pl.ds(8 * part, 8), :],
                        dz_out.at[pl.ds(2 * h, 2), slot, :, :, pl.ds(8 * part, 8), :],
                        y3s.at[h, part, d - 1], y3r.at[h, part, d - 1], y_peers[d],
                    )
                    for d in range(1, 8)
                ]
                for part in range(2)
            ]
        )
        keep_dz.append(pltpu.make_async_copy(dz_send.at[h, :, slot], home, keep_sem.at[h, 5]))

    for u in range(CHUNKS):
        h, e = u // 2, u % 2
        if e == 0:
            for copy in loads[3 * h : 3 * h + 3]:
                copy.wait()

        @pl.loop(0, 5)
        def _(f):
            for k in range(4):
                planes = own[h, f, pl.ds(2 * k + e, ROWS, stride=PLANES), :]
                apart[u, :, k, f] = planes.reshape(GROUPS, HOLD, LANES)

        if u == 0:
            pl.semaphore_wait(barrier, 12)
        for copy in z1[u]:
            copy.start()
        for copy in x1[u]:
            copy.start()
        for copy in y1[u]:
            copy.start()
        keeps[u][0].start()
        keeps[u][2].start()

    load_wall.start()

    load_wall.wait()

    @pl.loop(0, HALF // 64)
    def _(i):
        rows = pl.ds(i * 64, 64)
        high, low = split(wall_f[rows, :])
        wall_h[rows, :] = high
        wall_l[rows, :] = low

    high, low = [
        dot(order_out[z_hi], dot(part, order_in[...]).astype(jnp.bfloat16)).astype(jnp.bfloat16) for part in split(span[...])
    ]
    span_2[0 : NZ // 2, 0:NZ] = high
    span_2[0 : NZ // 2, NZ : 2 * NZ] = high
    span_2[NZ // 2 : NZ, 0:NZ] = low
    span_2[NZ // 2 : NZ, NZ : 2 * NZ] = jnp.zeros((NZ // 2, NZ), jnp.bfloat16)
    for u in range(CHUNKS):
        for f in range(5):
            for group in (0, NY // HOLD + 1):
                lines_y[u, group, f] = jnp.zeros((HOLD, LANES), jnp.float32)

    @pl.loop(0, ROWS * PLANES // 64)
    def _(i):
        rows = pl.ds(i * 64, 64)
        c = [jnp.concatenate([own[0, f, rows, :], own[1, f, rows, :]], axis=1) for f in range(5)]
        for f, value in enumerate(flux_along(c, 0)):
            high, low = split(value)
            along = (dot(high, shift[...]) + dot(low, shift[...])) * (1.0 / 12.0)
            value = c[f] - TIME_STEP * along
            for h in range(2):
                own[h, f, rows, :] = value[:, h * LANES : (h + 1) * LANES]

    def pass_near(u, j):
        z1[u][j].wait_recv()
        z2[u][j].start()
        if j == 1:
            for copy in x2[u]:
                copy.start()
            keeps[u][1].start()

    def pass_far(u, j):
        z2[u][j].wait_recv()
        for copy in y2[u][j]:
            copy.start()
        if j == 1:
            keeps[u][3].start()

    def derive_y(u):
        keeps[u][0].wait()
        keeps[u][1].wait()
        for copy in x1[u] + x2[u]:
            copy.wait_recv()

        @pl.loop(0, NY // 64)
        def _(i):
            r = pl.multiple_of(i * 64, 64)
            c = [lines_y[u, pl.ds(1 + i * 4, 4), f].reshape(64, LANES) for f in range(5)]
            for f, value in enumerate(flux_along(c, 1)):
                high, low = split(value)
                flux_h[pl.ds(r, 64), f * LANES : (f + 1) * LANES] = high
                flux_l[pl.ds(r, 64), f * LANES : (f + 1) * LANES] = low

        @pl.loop(0, 4)
        def _(k):
            rows = pl.ds(pl.multiple_of(k * ROWS, ROWS), ROWS)
            total = dot(wall_h[rows, :], flux_h[...])
            total += dot(wall_h[rows, :], flux_l[...])
            total += dot(wall_l[rows, :], flux_h[...])
            block = z_lo * 4 + k
            weight = jnp.broadcast_to(damp_rows[pl.ds(block, 1), :], (ROWS, LANES)).T
            for f in range(5):
                window = lines_y[u, pl.ds(block * GROUPS, GROUPS + 2), f].reshape(ROWS + 2 * HOLD, LANES)

                def at(step, window=window):
                    return window[HOLD + step : HOLD + step + ROWS]

                smooth = at(-2) - 4.0 * at(-1) + 6.0 * at(0) - 4.0 * at(1) + at(2)
                total_f = total[:, f * LANES : (f + 1) * LANES] + weight * smooth
                dy_send[u, k, :, f] = total_f.reshape(GROUPS, HOLD, LANES)

        for copy in x3[u]:
            copy.start()
        keeps[u][4].start()

    def derive_z(h):
        for u in (2 * h, 2 * h + 1):
            keeps[u][2].wait()
            keeps[u][3].wait()
            for copy in y1[u] + y2[u][0] + y2[u][1]:
                copy.wait_recv()
        lines = lines_z.reshape(CHUNKS, GZ * 4 * 5 * HOLD, LANES)
        results = dz_send.reshape(2, 2 * 8 * 4 * 5 * HOLD, LANES)

        for part in range(2):

            @pl.loop(8 * part, 8 * part + 8, unroll=2)
            def _(r):
                weight = damp[gy * ROWS + slot * HOLD + r]
                c = []
                for f in range(5):
                    at = pl.ds(f * HOLD + r, NZ // 2, stride=5 * HOLD)
                    c.append(jnp.concatenate([lines[2 * h, at, :], lines[2 * h + 1, at, :]], axis=0))
                high, low = split(jnp.concatenate(flux_along(c, 2), axis=1))
                both = dot(span_2[...], jnp.concatenate([high, low], axis=0))
                high, low = split(jnp.concatenate(c, axis=1))
                total = weight * dot(fourth[z_hi], jnp.concatenate([high, low], axis=0))
                total += both[0 : NZ // 2] + both[NZ // 2 :]
                for f in range(5):
                    at = pl.ds(f * HOLD + r, NZ // 2, stride=5 * HOLD)
                    results[h, at, :] = total[:, f * LANES : (f + 1) * LANES]

            for copy in y3[h][part]:
                copy.start()
        keep_dz[h].start()

    def add(h, f, source):
        for e in range(2):
            for k in range(4):
                at = pl.ds(2 * k + e, ROWS, stride=PLANES)
                part = source(2 * h + e, k).reshape(ROWS, LANES)
                own[h, f, at, :] = own[h, f, at, :] - TIME_STEP * part

    def add_y(h):
        for u in (2 * h, 2 * h + 1):
            keeps[u][4].wait()
            for copy in x3[u]:
                copy.wait_recv()

        @pl.loop(0, 5)
        def _(f):
            add(h, f, lambda u, k: dy_out[u, k, :, f])

    saves = [
        [pltpu.make_async_copy(own.at[h, f], new_out.at[h, f], save_sem.at[h, f]) for f in range(5)] for h in range(2)
    ]

    def add_z(h):
        keep_dz[h].wait()
        for copy in y3[h][0] + y3[h][1]:
            copy.wait_recv()
        for f in range(5):
            add(h, f, lambda u, k, f=f: dz_out[u, :, k, f])
            saves[h][f].start()

    pass_near(0, 0)
    pass_near(0, 1)
    pass_far(0, 0)
    pass_near(1, 0)
    pass_far(0, 1)
    pass_near(1, 1)
    pass_far(1, 0)
    pass_near(2, 0)
    pass_far(1, 1)
    derive_y(0)
    pass_near(2, 1)
    pass_far(2, 0)
    derive_z(0)
    derive_y(1)
    pass_near(3, 0)
    pass_far(2, 1)
    pass_near(3, 1)
    pass_far(3, 0)
    derive_y(2)
    pass_far(3, 1)
    derive_z(1)
    derive_y(3)
    add_y(0)
    add_z(0)
    add_y(1)
    add_z(1)

    for h in range(2):
        for copy in y3[h][0] + y3[h][1]:
            copy.wait_send()
    for u in range(CHUNKS):
        for copy in z1[u] + z2[u] + x1[u] + x2[u] + x3[u] + y1[u] + y2[u][0] + y2[u][1]:
            copy.wait_send()
    for copy in saves[0] + saves[1]:
        copy.wait()


def join(halves, new_dens, new_mom, new_ene, whole, in_sem, out_sem):
    targets = [new_dens, new_mom.at[0], new_mom.at[1], new_mom.at[2], new_ene]
    ins = [
        [
            pltpu.make_async_copy(halves.at[h, f], whole.at[f, :, pl.ds(h * LANES, LANES)], in_sem.at[f, h])
            for h in range(2)
        ]
        for f in range(5)
    ]
    outs = [pltpu.make_async_copy(whole.at[f], targets[f], out_sem.at[f]) for f in range(5)]
    for f in range(5):
        for copy in ins[f]:
            copy.start()
    for f in range(5):
        for copy in ins[f]:
            copy.wait()
        outs[f].start()
    for copy in outs:
        copy.wait()


def plane_order():
    return np.arange(NZ).reshape(GZ, 4, 2).transpose(2, 0, 1).reshape(-1)


def half_order(z_hi):
    return np.arange(NZ).reshape(4, 2, 2, 4, 2)[:, z_hi].transpose(3, 0, 1, 2).reshape(-1)


def order_matrices():
    eye = np.eye(NZ, dtype=np.float32)
    return eye[:, plane_order()], np.stack([eye[half_order(z)] for z in range(2)])


def fourth_matrix():
    m = np.zeros((NZ, NZ), np.float32)
    for i in range(NZ):
        for k, w in ((-2, 1.0), (-1, -4.0), (0, 6.0), (1, -4.0), (2, 1.0)):
            m[i, (i + k) % NZ] += w
    m = np.stack([m[half_order(z)][:, plane_order()] for z in range(2)])
    return np.concatenate([m, m], axis=2)


def shift_matrix():
    m = np.zeros((CELLS, CELLS), np.float32)
    for i in range(CELLS):
        for k, w in ((1, 8.0), (-1, -8.0), (2, -1.0), (-2, 1.0)):
            m[min(max(i + k, 0), CELLS - 1), i] += w
    return m


ANY = pl.BlockSpec(memory_space=pl.ANY)
VMEM = pl.BlockSpec(memory_space=pltpu.VMEM)
SMEM = pl.BlockSpec(memory_space=pltpu.SMEM)
DMA = pltpu.SemaphoreType.DMA


def local(density, momentum, energy, wall_operator, span_operator, damping):
    cells = ROWS * PLANES
    dens = density.reshape(cells, CELLS)
    mom = momentum.reshape(3, cells, CELLS)
    ene = energy.reshape(cells, CELLS)
    f32, bf16 = jnp.float32, jnp.bfloat16
    order_in, order_out = order_matrices()
    whole = jax.ShapeDtypeStruct((CHUNKS, GROUPS, 4, 5, HOLD, LANES), f32)
    halves, _, _ = pl.pallas_call(
        exchange,
        out_shape=(jax.ShapeDtypeStruct((2, 5, cells, LANES), f32), whole, whole),
        in_specs=[ANY, ANY, ANY, ANY, VMEM, SMEM, VMEM, VMEM, VMEM, VMEM, VMEM],
        out_specs=(ANY,) * 3,
        scratch_shapes=[
            pltpu.VMEM((CHUNKS, 4, GROUPS, 5, HOLD, LANES), f32),
            pltpu.VMEM((CHUNKS, GROUPS, 4, 5, HOLD, LANES), f32),
            pltpu.VMEM((2, 5, cells, LANES), f32),
            pltpu.VMEM((CHUNKS, GROUPS, 4, 5, HOLD, LANES), f32),
            pltpu.VMEM((CHUNKS, NY // HOLD + 2, 5, HOLD, LANES), f32),
            pltpu.VMEM((CHUNKS, GZ, 4, 5, HOLD, LANES), f32),
            pltpu.VMEM((CHUNKS, 4, GROUPS, 5, HOLD, LANES), f32),
            pltpu.VMEM((2, 2, 8, 4, 5, HOLD, LANES), f32),
            pltpu.VMEM((HALF, NY), f32),
            pltpu.VMEM((HALF, NY), bf16),
            pltpu.VMEM((HALF, NY), bf16),
            pltpu.VMEM((NY, 5 * LANES), bf16),
            pltpu.VMEM((NY, 5 * LANES), bf16),
            pltpu.VMEM((NZ, 2 * NZ), bf16),
            *[DMA((CHUNKS, 2))] * 4,
            *[DMA((CHUNKS, 3))] * 6,
            *[DMA((CHUNKS, 7))] * 2,
            *[DMA((CHUNKS, 2, 7))] * 2,
            *[DMA((2, 2, 7))] * 2,
            DMA((7,)),
            DMA((CHUNKS, 6)),
            DMA((2, 5)),
        ],
        compiler_params=pltpu.CompilerParams(
            collective_id=0, has_side_effects=True, vmem_limit_bytes=62 << 20
        ),
        name="exchange",
    )(
        dens, mom, ene, wall_operator, span_operator, damping, damping.reshape(GY, ROWS),
        jnp.asarray(fourth_matrix(), bf16), jnp.asarray(order_in, bf16), jnp.asarray(order_out, bf16),
        jnp.asarray(shift_matrix(), bf16),
    )
    new = pl.pallas_call(
        join,
        out_shape=(
            jax.ShapeDtypeStruct((cells, CELLS), f32),
            jax.ShapeDtypeStruct((3, cells, CELLS), f32),
            jax.ShapeDtypeStruct((cells, CELLS), f32),
        ),
        in_specs=[ANY],
        out_specs=(ANY,) * 3,
        scratch_shapes=[pltpu.VMEM((5, cells, CELLS), f32), DMA((5, 2)), DMA((5,))],
        name="join",
    )(halves)
    shape = (ROWS, PLANES, CELLS)
    return new[0].reshape(shape), new[1].reshape((3,) + shape), new[2].reshape(shape)


def solution(mesh):
    in_specs = (P("gy", "gz", None), P(None, "gy", "gz", None), P("gy", "gz", None), P(), P(), P())
    out_specs = (P("gy", "gz", None), P(None, "gy", "gz", None), P("gy", "gz", None))
    return jax.shard_map(local, mesh=mesh, in_specs=in_specs, out_specs=out_specs, check_vma=False)
```

```python
import functools

import jax
import jax.numpy as jnp
import numpy as np
from jax import lax
from jax.experimental import pallas as pl
from jax.experimental.pallas import tpu as pltpu
from jax.sharding import PartitionSpec as P

MESH = pl.DeviceIdType.MESH
GAMMA_LESS = 0.4
TIME_STEP = 0.1
GY, GZ = 8, 16
ROWS, PLANES, CELLS, LANES = 128, 8, 256, 128
NY, NZ = GY * ROWS, GZ * PLANES
HOLD = 16
CHUNKS = 4
HALF = NY // 2
GROUPS = ROWS // HOLD


def flux_along(c, direction):
    inverse = 1.0 / c[0]
    velocity = c[1 + direction] * inverse
    kinetic = 0.5 * (c[1] * c[1] + c[2] * c[2] + c[3] * c[3]) * inverse
    pressure = GAMMA_LESS * (c[4] - kinetic)
    out = [c[1 + direction]]
    for column in range(3):
        product = c[1 + column] * velocity
        if column == direction:
            product = product + pressure
        out.append(product)
    out.append((c[4] + pressure) * velocity)
    return out


def split(x):
    high = x.astype(jnp.bfloat16)
    low = (x - high.astype(jnp.float32)).astype(jnp.bfloat16)
    return high, low


def dot(a, b):
    return jnp.dot(a, b, preferred_element_type=jnp.float32)


def exchange(
    dens, mom, ene, wall, span, damp, damp_rows, fourth, order_in, order_out, shift,
    new_out, near, far,
    dy_out, dz_out, own, apart, lines_y, lines_z, dy_send, dz_send, wall_f, wall_h, wall_l, flux_h, flux_l, span_2,
    z1s, z1r, z2s, z2r, x1s, x1r, x2s, x2r, x3s, x3r, y1s, y1r, y2s, y2r, y3s, y3r, load_sem, keep_sem, save_sem,
):
    gy = lax.axis_index("gy")
    gz = lax.axis_index("gz")
    z_lo, x = gy // 4, lax.rem(gy, 4)
    y, z_hi, core = gz // 4, lax.rem(gz // 2, 2), lax.rem(gz, 2)
    slot = y * 2 + core
    pair = ((1 - z_lo) * 4 + x, gz)
    relay = ((1 - z_lo) * 4 + x, y * 4 + (1 - z_hi) * 2 + core)
    x_of = [lax.rem(x + d, 4) for d in range(4)]
    x_peers = [(z_lo * 4 + other, gz) for other in x_of]
    slot_of = [lax.rem(slot + d, 8) for d in range(8)]
    y_peers = [(gy, (other // 2) * 4 + z_hi * 2 + lax.rem(other, 2)) for other in slot_of]
    far_gz = y * 4 + (1 - z_hi) * 2 + core
    near_group = 1 + gy * GROUPS
    far_group = 1 + pair[0] * GROUPS

    def send(src, dst, ssem, rsem, peer):
        return pltpu.make_async_remote_copy(src, dst, ssem, rsem, device_id=peer, device_id_type=MESH)

    loads = []
    for h in range(2):
        lanes = pl.ds(h * LANES, LANES)
        loads += [
            pltpu.make_async_copy(dens.at[:, lanes], own.at[h, 0], load_sem.at[3 * h]),
            pltpu.make_async_copy(mom.at[:, :, lanes], own.at[h, pl.ds(1, 3)], load_sem.at[3 * h + 1]),
            pltpu.make_async_copy(ene.at[:, lanes], own.at[h, 4], load_sem.at[3 * h + 2]),
        ]
    load_wall = pltpu.make_async_copy(wall.at[pl.ds(z_lo * HALF, HALF), :], wall_f, load_sem.at[6])
    for copy in loads:
        copy.start()

    barrier = pltpu.get_barrier_semaphore()
    for peer in [pair, relay] + x_peers[1:] + y_peers[1:]:
        pl.semaphore_signal(barrier, inc=1, device_id=peer, device_id_type=MESH)

    z1, z2 = [], []
    for u in range(CHUNKS):
        for copies, source, target, ssem, rsem, peer in (
            (z1, apart, near, z1s, z1r, pair),
            (z2, near, far, z2s, z2r, relay),
        ):
            copies.append(
                [
                    send(source.at[u, :, pl.ds(2 * j, 2)], target.at[u, :, pl.ds(2 * j, 2)], ssem.at[u, j], rsem.at[u, j], peer)
                    for j in range(2)
                ]
            )
    x1, x2, x3, keeps = [], [], [], []
    for u in range(CHUNKS):
        for copies, source, group, ssem, rsem in ((x1, apart, near_group, x1s, x1r), (x2, near, far_group, x2s, x2r)):
            target = lines_y.at[u, pl.ds(group, GROUPS)]
            copies.append(
                [
                    send(source.at[u, :, x_of[d]], target, ssem.at[u, d - 1], rsem.at[u, d - 1], x_peers[d])
                    for d in range(1, 4)
                ]
            )
        x3.append(
            [
                send(dy_send.at[u, x_of[d]], dy_out.at[u, x], x3s.at[u, d - 1], x3r.at[u, d - 1], x_peers[d])
                for d in range(1, 4)
            ]
        )
        keeps.append(
            [
                pltpu.make_async_copy(apart.at[u, :, x], lines_y.at[u, pl.ds(near_group, GROUPS)], keep_sem.at[u, 0]),
                pltpu.make_async_copy(near.at[u, :, x], lines_y.at[u, pl.ds(far_group, GROUPS)], keep_sem.at[u, 1]),
                pltpu.make_async_copy(
                    apart.at[u, slot], lines_z.at[u, gz], keep_sem.at[u, 2]
                ),
                pltpu.make_async_copy(
                    far.at[u, slot], lines_z.at[u, far_gz], keep_sem.at[u, 3]
                ),
                pltpu.make_async_copy(dy_send.at[u, x], dy_out.at[u, x], keep_sem.at[u, 4]),
            ]
        )
    y1, y2, y3, keep_dz = [], [], [], []
    for u in range(CHUNKS):
        y1.append(
            [
                send(
                    apart.at[u, slot_of[d]], lines_z.at[u, gz],
                    y1s.at[u, d - 1], y1r.at[u, d - 1], y_peers[d],
                )
                for d in range(1, 8)
            ]
        )
        y2.append(
            [
                [
                    send(
                        far.at[u, slot_of[d], pl.ds(2 * j, 2)],
                        lines_z.at[u, far_gz, pl.ds(2 * j, 2)],
                        y2s.at[u, j, d - 1], y2r.at[u, j, d - 1], y_peers[d],
                    )
                    for d in range(1, 8)
                ]
                for j in range(2)
            ]
        )
    for h in range(2):
        home = dz_out.at[pl.ds(2 * h, 2), slot]
        y3.append(
            [
                [
                    send(
                        dz_send.at[h, :, slot_of[d], :, :, pl.ds(8 * part, 8), :],
                        dz_out.at[pl.ds(2 * h, 2), slot, :, :, pl.ds(8 * part, 8), :],
                        y3s.at[h, part, d - 1], y3r.at[h, part, d - 1], y_peers[d],
                    )
                    for d in range(1, 8)
                ]
                for part in range(2)
            ]
        )
        keep_dz.append(pltpu.make_async_copy(dz_send.at[h, :, slot], home, keep_sem.at[h, 5]))

    for u in range(CHUNKS):
        h, e = u // 2, u % 2
        if e == 0:
            for copy in loads[3 * h : 3 * h + 3]:
                copy.wait()

        @pl.loop(0, 5)
        def _(f):
            for k in range(4):
                planes = own[h, f, pl.ds(2 * k + e, ROWS, stride=PLANES), :]
                apart[u, :, k, f] = planes.reshape(GROUPS, HOLD, LANES)

        if u == 0:
            pl.semaphore_wait(barrier, 12)
        for copy in z1[u]:
            copy.start()
        for copy in x1[u]:
            copy.start()
        for copy in y1[u]:
            copy.start()
        keeps[u][0].start()
        keeps[u][2].start()

    load_wall.start()

    load_wall.wait()

    @pl.loop(0, HALF // 64)
    def _(i):
        rows = pl.ds(i * 64, 64)
        high, low = split(wall_f[rows, :])
        wall_h[rows, :] = high
        wall_l[rows, :] = low

    high, low = [
        dot(order_out[z_hi], dot(part, order_in[...]).astype(jnp.bfloat16)).astype(jnp.bfloat16) for part in split(span[...])
    ]
    span_2[0 : NZ // 2, 0:NZ] = high
    span_2[0 : NZ // 2, NZ : 2 * NZ] = high
    span_2[NZ // 2 : NZ, 0:NZ] = low
    span_2[NZ // 2 : NZ, NZ : 2 * NZ] = jnp.zeros((NZ // 2, NZ), jnp.bfloat16)
    for u in range(CHUNKS):
        for f in range(5):
            for group in (0, NY // HOLD + 1):
                lines_y[u, group, f] = jnp.zeros((HOLD, LANES), jnp.float32)

    @pl.loop(0, ROWS * PLANES // 64)
    def _(i):
        rows = pl.ds(i * 64, 64)
        c = [jnp.concatenate([own[0, f, rows, :], own[1, f, rows, :]], axis=1) for f in range(5)]
        for f, value in enumerate(flux_along(c, 0)):
            high, low = split(value)
            along = (dot(high, shift[...]) + dot(low, shift[...])) * (1.0 / 12.0)
            value = c[f] - TIME_STEP * along
            for h in range(2):
                own[h, f, rows, :] = value[:, h * LANES : (h + 1) * LANES]

    def pass_near(u, j):
        z1[u][j].wait_recv()
        z2[u][j].start()
        if j == 1:
            for copy in x2[u]:
                copy.start()
            keeps[u][1].start()

    def pass_far(u, j):
        z2[u][j].wait_recv()
        for copy in y2[u][j]:
            copy.start()
        if j == 1:
            keeps[u][3].start()

    def derive_y(u):
        keeps[u][0].wait()
        keeps[u][1].wait()
        for copy in x1[u] + x2[u]:
            copy.wait_recv()

        @pl.loop(0, NY // 64)
        def _(i):
            r = pl.multiple_of(i * 64, 64)
            c = [lines_y[u, pl.ds(1 + i * 4, 4), f].reshape(64, LANES) for f in range(5)]
            for f, value in enumerate(flux_along(c, 1)):
                high, low = split(value)
                flux_h[pl.ds(r, 64), f * LANES : (f + 1) * LANES] = high
                flux_l[pl.ds(r, 64), f * LANES : (f + 1) * LANES] = low

        @pl.loop(0, 4)
        def _(k):
            rows = pl.ds(pl.multiple_of(k * ROWS, ROWS), ROWS)
            total = dot(wall_h[rows, :], flux_h[...])
            total += dot(wall_h[rows, :], flux_l[...])
            total += dot(wall_l[rows, :], flux_h[...])
            block = z_lo * 4 + k
            weight = jnp.broadcast_to(damp_rows[pl.ds(block, 1), :], (ROWS, LANES)).T
            for f in range(5):
                window = lines_y[u, pl.ds(block * GROUPS, GROUPS + 2), f].reshape(ROWS + 2 * HOLD, LANES)

                def at(step, window=window):
                    return window[HOLD + step : HOLD + step + ROWS]

                smooth = at(-2) - 4.0 * at(-1) + 6.0 * at(0) - 4.0 * at(1) + at(2)
                total_f = total[:, f * LANES : (f + 1) * LANES] + weight * smooth
                dy_send[u, k, :, f] = total_f.reshape(GROUPS, HOLD, LANES)

        for copy in x3[u]:
            copy.start()
        keeps[u][4].start()

    def derive_z(h):
        for u in (2 * h, 2 * h + 1):
            keeps[u][2].wait()
            keeps[u][3].wait()
            for copy in y1[u] + y2[u][0] + y2[u][1]:
                copy.wait_recv()
        lines = lines_z.reshape(CHUNKS, GZ * 4 * 5 * HOLD, LANES)
        results = dz_send.reshape(2, 2 * 8 * 4 * 5 * HOLD, LANES)

        for part in range(2):

            @pl.loop(8 * part, 8 * part + 8, unroll=2)
            def _(r):
                weight = damp[gy * ROWS + slot * HOLD + r]
                c = []
                for f in range(5):
                    at = pl.ds(f * HOLD + r, NZ // 2, stride=5 * HOLD)
                    c.append(jnp.concatenate([lines[2 * h, at, :], lines[2 * h + 1, at, :]], axis=0))
                high, low = split(jnp.concatenate(flux_along(c, 2), axis=1))
                both = dot(span_2[...], jnp.concatenate([high, low], axis=0))
                high, low = split(jnp.concatenate(c, axis=1))
                total = weight * dot(fourth[z_hi], jnp.concatenate([high, low], axis=0))
                total += both[0 : NZ // 2] + both[NZ // 2 :]
                for f in range(5):
                    at = pl.ds(f * HOLD + r, NZ // 2, stride=5 * HOLD)
                    results[h, at, :] = total[:, f * LANES : (f + 1) * LANES]

            for copy in y3[h][part]:
                copy.start()
        keep_dz[h].start()

    def add(h, f, source):
        for e in range(2):
            for k in range(4):
                at = pl.ds(2 * k + e, ROWS, stride=PLANES)
                part = source(2 * h + e, k).reshape(ROWS, LANES)
                own[h, f, at, :] = own[h, f, at, :] - TIME_STEP * part

    def add_y(h):
        for u in (2 * h, 2 * h + 1):
            keeps[u][4].wait()
            for copy in x3[u]:
                copy.wait_recv()

        @pl.loop(0, 5)
        def _(f):
            add(h, f, lambda u, k: dy_out[u, k, :, f])

    saves = [
        [pltpu.make_async_copy(own.at[h, f], new_out.at[h, f], save_sem.at[h, f]) for f in range(5)] for h in range(2)
    ]

    def add_z(h):
        keep_dz[h].wait()
        for copy in y3[h][0] + y3[h][1]:
            copy.wait_recv()
        for f in range(5):
            add(h, f, lambda u, k, f=f: dz_out[u, :, k, f])
            saves[h][f].start()

    pass_near(0, 0)
    pass_near(0, 1)
    pass_far(0, 0)
    pass_near(1, 0)
    pass_far(0, 1)
    pass_near(1, 1)
    pass_far(1, 0)
    pass_near(2, 0)
    pass_far(1, 1)
    derive_y(0)
    pass_near(2, 1)
    pass_far(2, 0)
    derive_z(0)
    derive_y(1)
    pass_near(3, 0)
    pass_far(2, 1)
    pass_near(3, 1)
    pass_far(3, 0)
    pass_far(3, 1)
    derive_y(2)
    derive_z(1)
    derive_y(3)
    add_y(0)
    add_z(0)
    add_y(1)
    add_z(1)

    for h in range(2):
        for copy in y3[h][0] + y3[h][1]:
            copy.wait_send()
    for u in range(CHUNKS):
        for copy in z1[u] + z2[u] + x1[u] + x2[u] + x3[u] + y1[u] + y2[u][0] + y2[u][1]:
            copy.wait_send()
    for copy in saves[0] + saves[1]:
        copy.wait()


def join(halves, new_dens, new_mom, new_ene, whole, in_sem, out_sem):
    targets = [new_dens, new_mom.at[0], new_mom.at[1], new_mom.at[2], new_ene]
    ins = [
        [
            pltpu.make_async_copy(halves.at[h, f], whole.at[f, :, pl.ds(h * LANES, LANES)], in_sem.at[f, h])
            for h in range(2)
        ]
        for f in range(5)
    ]
    outs = [pltpu.make_async_copy(whole.at[f], targets[f], out_sem.at[f]) for f in range(5)]
    for f in range(5):
        for copy in ins[f]:
            copy.start()
    for f in range(5):
        for copy in ins[f]:
            copy.wait()
        outs[f].start()
    for copy in outs:
        copy.wait()


def plane_order():
    return np.arange(NZ).reshape(GZ, 4, 2).transpose(2, 0, 1).reshape(-1)


def half_order(z_hi):
    return np.arange(NZ).reshape(4, 2, 2, 4, 2)[:, z_hi].transpose(3, 0, 1, 2).reshape(-1)


def order_matrices():
    eye = np.eye(NZ, dtype=np.float32)
    return eye[:, plane_order()], np.stack([eye[half_order(z)] for z in range(2)])


def fourth_matrix():
    m = np.zeros((NZ, NZ), np.float32)
    for i in range(NZ):
        for k, w in ((-2, 1.0), (-1, -4.0), (0, 6.0), (1, -4.0), (2, 1.0)):
            m[i, (i + k) % NZ] += w
    m = np.stack([m[half_order(z)][:, plane_order()] for z in range(2)])
    return np.concatenate([m, m], axis=2)


def shift_matrix():
    m = np.zeros((CELLS, CELLS), np.float32)
    for i in range(CELLS):
        for k, w in ((1, 8.0), (-1, -8.0), (2, -1.0), (-2, 1.0)):
            m[min(max(i + k, 0), CELLS - 1), i] += w
    return m


ANY = pl.BlockSpec(memory_space=pl.ANY)
VMEM = pl.BlockSpec(memory_space=pltpu.VMEM)
SMEM = pl.BlockSpec(memory_space=pltpu.SMEM)
DMA = pltpu.SemaphoreType.DMA


def local(density, momentum, energy, wall_operator, span_operator, damping):
    cells = ROWS * PLANES
    dens = density.reshape(cells, CELLS)
    mom = momentum.reshape(3, cells, CELLS)
    ene = energy.reshape(cells, CELLS)
    f32, bf16 = jnp.float32, jnp.bfloat16
    order_in, order_out = order_matrices()
    whole = jax.ShapeDtypeStruct((CHUNKS, GROUPS, 4, 5, HOLD, LANES), f32)
    halves, _, _ = pl.pallas_call(
        exchange,
        out_shape=(jax.ShapeDtypeStruct((2, 5, cells, LANES), f32), whole, whole),
        in_specs=[ANY, ANY, ANY, ANY, VMEM, SMEM, VMEM, VMEM, VMEM, VMEM, VMEM],
        out_specs=(ANY,) * 3,
        scratch_shapes=[
            pltpu.VMEM((CHUNKS, 4, GROUPS, 5, HOLD, LANES), f32),
            pltpu.VMEM((CHUNKS, GROUPS, 4, 5, HOLD, LANES), f32),
            pltpu.VMEM((2, 5, cells, LANES), f32),
            pltpu.VMEM((CHUNKS, GROUPS, 4, 5, HOLD, LANES), f32),
            pltpu.VMEM((CHUNKS, NY // HOLD + 2, 5, HOLD, LANES), f32),
            pltpu.VMEM((CHUNKS, GZ, 4, 5, HOLD, LANES), f32),
            pltpu.VMEM((CHUNKS, 4, GROUPS, 5, HOLD, LANES), f32),
            pltpu.VMEM((2, 2, 8, 4, 5, HOLD, LANES), f32),
            pltpu.VMEM((HALF, NY), f32),
            pltpu.VMEM((HALF, NY), bf16),
            pltpu.VMEM((HALF, NY), bf16),
            pltpu.VMEM((NY, 5 * LANES), bf16),
            pltpu.VMEM((NY, 5 * LANES), bf16),
            pltpu.VMEM((NZ, 2 * NZ), bf16),
            *[DMA((CHUNKS, 2))] * 4,
            *[DMA((CHUNKS, 3))] * 6,
            *[DMA((CHUNKS, 7))] * 2,
            *[DMA((CHUNKS, 2, 7))] * 2,
            *[DMA((2, 2, 7))] * 2,
            DMA((7,)),
            DMA((CHUNKS, 6)),
            DMA((2, 5)),
        ],
        compiler_params=pltpu.CompilerParams(
            collective_id=0, has_side_effects=True, vmem_limit_bytes=62 << 20
        ),
        name="exchange",
    )(
        dens, mom, ene, wall_operator, span_operator, damping, damping.reshape(GY, ROWS),
        jnp.asarray(fourth_matrix(), bf16), jnp.asarray(order_in, bf16), jnp.asarray(order_out, bf16),
        jnp.asarray(shift_matrix(), bf16),
    )
    new = pl.pallas_call(
        join,
        out_shape=(
            jax.ShapeDtypeStruct((cells, CELLS), f32),
            jax.ShapeDtypeStruct((3, cells, CELLS), f32),
            jax.ShapeDtypeStruct((cells, CELLS), f32),
        ),
        in_specs=[ANY],
        out_specs=(ANY,) * 3,
        scratch_shapes=[pltpu.VMEM((5, cells, CELLS), f32), DMA((5, 2)), DMA((5,))],
        name="join",
    )(halves)
    shape = (ROWS, PLANES, CELLS)
    return new[0].reshape(shape), new[1].reshape((3,) + shape), new[2].reshape(shape)


def solution(mesh):
    in_specs = (P("gy", "gz", None), P(None, "gy", "gz", None), P("gy", "gz", None), P(), P(), P())
    out_specs = (P("gy", "gz", None), P(None, "gy", "gz", None), P("gy", "gz", None))
    return jax.shard_map(local, mesh=mesh, in_specs=in_specs, out_specs=out_specs, check_vma=False)
```
